32 devices in a mesh: ctx: 8 (over y, x, core), tp: 4 (over z).
Axes of the slice: x: 2, y: 2, z: 4, core: 2. Of those that a mesh axis runs over, the one named last changes fastest.
Arguments:
- tokens: bfloat16 [4096, 4096], P('ctx', 'tp'), may hold values from -6 to 6
- norm_gain: float32 [4096], replicated, may hold values from 0.5 to 1.5
- proj_weight: bfloat16 [3, 4096, 2048], P(None, None, 'tp'), may hold values from -0.09375 to 0.09375
- short_taps: float32 [3, 3, 2048], P(None, None, 'tp'), may hold values from -1 to 1
- long_filter: float32 [4096, 2048], P('ctx', 'tp'), may hold values from -0.09375 to 0.09375
- skip_gain: float32 [2048], P('tp'), may hold values from -1 to 1
Outputs:
- output: bfloat16 [4096, 2048], P('ctx', 'tp')
The draws below stay inside these ranges and needn't reach their ends.
All inputs are finite; a program needn't handle non-finite values.
Results may differ from the reference program's by a relative error of at most 0.0081.
Values may be sent and summed in bfloat16 or wider, within the bound.
A program may use at most 128 MiB of HBM per device.

```python
import jax
import jax.numpy as jnp
from jax import lax

D = 4096
CH = 2048
SEQ = 4096
N_TP = 4


def level_of(stream_key, dims, cuts, smallest, largest):
    factor_of = 1.0
    for position, blocks in cuts:
        heights = jax.random.uniform(jax.random.fold_in(jax.random.fold_in(stream_key, 6), position), (blocks,), jnp.float32, smallest / len(cuts), largest / len(cuts))
        factor_of = factor_of * jnp.repeat(jnp.exp(heights), dims[position] // blocks).reshape((-1,) + (1,) * (len(dims) - 1 - position))
    return factor_of


def noise(rng, dims, scale, bound, cuts=(), held_as=jnp.bfloat16):
    entries = jax.random.normal(rng, dims, jnp.float32) * scale
    if len(cuts) > 0:
        entries = level_of(rng, dims, cuts, -0.22, 0.18) * entries
    return jnp.clip(entries, min=-bound, max=bound).astype(held_as)


def setup_inputs(seed: int = 0) -> dict:
    arg_keys = jax.random.split(jax.random.key(seed), 7)
    tokens = noise(arg_keys[0], (SEQ, D), 1.0, 6.0, ((0, 8), (1, 4)))
    norm_gain = jnp.clip(1.0 + 0.1 * jax.random.normal(arg_keys[1], (D,), jnp.float32), 0.5, 1.5)
    proj_weight = noise(arg_keys[2], (3, D, CH), D ** -0.5, 0.09375, ((2, 4),))
    short_taps = jnp.clip(jax.random.uniform(arg_keys[3], (3, 3, CH), jnp.float32, -1.0, 1.0) * level_of(arg_keys[3], (3, 3, CH), ((2, 4),), -0.4, 0.0), -1.0, 1.0)
    long_filter = noise(arg_keys[4], (SEQ, CH), SEQ ** -0.5, 0.09375, ((0, 8), (1, 4)), jnp.float32)
    skip_gain = jnp.clip(jax.random.uniform(arg_keys[5], (CH,), jnp.float32, -1.0, 1.0) * level_of(arg_keys[5], (CH,), ((0, 4),), -0.4, 0.0), -1.0, 1.0)
    return dict(tokens=tokens, norm_gain=norm_gain, proj_weight=proj_weight, short_taps=short_taps, long_filter=long_filter, skip_gain=skip_gain)


def reference(tokens, norm_gain, proj_weight, short_taps, long_filter, skip_gain):
    widened = tokens.astype(jnp.float32)
    scaling = lax.rsqrt(lax.optimization_barrier(jnp.mean(widened * widened, axis=1, keepdims=True)) + 1e-06)
    normed = (widened * scaling * norm_gain).astype(jnp.bfloat16)
    projected = jnp.stack([jnp.dot(normed, proj_weight[which], preferred_element_type=jnp.float32) for which in range(3)]).astype(jnp.bfloat16)
    padded = jnp.pad(projected.astype(jnp.float32), ((0, 0), (2, 0), (0, 0)))
    branch = short_taps[:, 0, None, :] * padded[:, 2:, :] + short_taps[:, 1, None, :] * padded[:, 1:-1, :] + short_taps[:, 2, None, :] * padded[:, :-2, :]
    mixed_field = branch[1] * branch[2]
    seq_length = tokens.shape[0]
    group_width = CH // N_TP
    group_count = CH // group_width

    def convolve(group_number):
        first = (group_number * group_width).astype(jnp.int32)
        signal = lax.dynamic_slice_in_dim(mixed_field, first, group_width, 1)
        impulse = lax.dynamic_slice_in_dim(long_filter, first, group_width, 1)
        spectrum = jnp.fft.rfft(signal, n=2 * seq_length, axis=0) * jnp.fft.rfft(impulse, n=2 * seq_length, axis=0)
        return jnp.fft.irfft(spectrum, n=2 * seq_length, axis=0)[:seq_length].astype(jnp.float32)
    pieces = lax.map(convolve, jnp.arange(group_count, dtype=jnp.int32))
    convolved = jnp.transpose(pieces, (1, 0, 2)).reshape(seq_length, CH)
    return (branch[0] * (convolved + skip_gain * mixed_field)).astype(jnp.bfloat16)
```

```python
import functools
import math

import jax
import jax.numpy as jnp
import numpy as np
from jax import lax
from jax.experimental import pallas as pl
from jax.experimental.pallas import tpu as pltpu
from jax.sharding import PartitionSpec as P

MESH = pl.DeviceIdType.MESH
EDGE = 16


def twist_tables(part_count, row_count):
    turn = np.arange(part_count + 1)[:, None] * np.arange(row_count)[None, :]
    angles = turn * (math.pi / (part_count * row_count))
    return np.cos(angles).astype(np.float32), np.sin(angles).astype(np.float32)


def inner_tables(row_count, halves):
    turn = np.arange(row_count)[:, None] * np.arange(row_count)[None, :] % row_count
    angles = turn * (2.0 * math.pi / row_count)
    cos, sin = np.cos(angles), np.sin(angles)
    forward = np.block([[cos, -sin], [sin, cos]])
    backward = np.block([[cos, sin], [-sin, cos]])
    part = row_count // halves
    backward = np.stack(
        [
            np.concatenate(
                [
                    backward[:, h * part : (h + 1) * part],
                    backward[:, row_count + h * part : row_count + (h + 1) * part],
                ],
                axis=1,
            )
            for h in range(halves)
        ]
    )
    return forward.astype(jnp.bfloat16), backward.astype(jnp.bfloat16)


def turn_of(a, k, part_count):
    step = a * k % (2 * part_count)
    cos = math.cos(math.pi * step / part_count)
    sin = math.sin(math.pi * step / part_count)
    return (0.0 if abs(cos) < 1e-12 else cos, 0.0 if abs(sin) < 1e-12 else sin)


def weighted(terms):
    total = None
    for factor, term in terms:
        if factor == 0.0:
            continue
        scaled = term if abs(factor - 1.0) < 1e-12 else -term if abs(factor + 1.0) < 1e-12 else factor * term
        total = scaled if total is None else total + scaled
    return total


def block_kernel(
    part_count, tp_count, chunk, halves,
    tokens_any, gain_ref, weight_any, taps_ref, filter_any, skip_ref, cos_ref, sin_ref, forward_any, backward_any,
    out_ref,
    held, weight, total, normed, scale, squares, filt, f_sent, f_got, turned, response, spec_turned,
    halo_out, halo_in, wide, gate, direct, x_sent, x_got, back, y_sent, y_got, forward, backward,
    load_sem, weight_sem, tok_send, tok_recv, sq_send, sq_recv, f_send, f_recv, halo_sem, x_send, x_recv, y_send, y_recv,
):
    row_count, width = out_ref.shape
    features = held.shape[2]
    channels = width // part_count
    chunks = row_count // chunk
    me = lax.axis_index("ctx")
    t = lax.axis_index("tp")
    upper = t // (tp_count // 2)
    u = t + upper * (tp_count - 1 - 2 * t)
    inward = 1 - 2 * upper
    middle = u == 1

    def mirrored(o):
        return o + upper * (tp_count - 1 - 2 * o)

    order = [t, mirrored(1 - u)] + [mirrored(k) for k in range(2, tp_count)]

    loads = [
        pltpu.make_async_copy(source, target, load_sem.at[i])
        for i, (source, target) in enumerate(
            [
                (tokens_any, held.at[t]),
                (filter_any, filt),
                (forward_any, forward),
                (backward_any, backward),
            ]
        )
    ]

    def weight_load(k):
        rows = pl.ds(pl.multiple_of(order[k] * features, features), features)
        return pltpu.make_async_copy(weight_any.at[:, rows, :], weight.at[:, rows, :], weight_sem.at[k])

    barrier = pltpu.get_barrier_semaphore()

    def greet_ctx(shift, _):
        pl.semaphore_signal(barrier, inc=1, device_id={"ctx": lax.rem(me + shift, part_count)}, device_id_type=MESH)
        return 0

    lax.fori_loop(1, part_count, greet_ctx, 0)
    for shift in range(1, tp_count):
        pl.semaphore_signal(barrier, inc=1, device_id={"tp": lax.rem(t + shift, tp_count)}, device_id_type=MESH)
    loads[0].start()
    loads[1].start()
    pl.semaphore_wait(barrier, part_count - 1 + tp_count - 1)

    pieces = (
        [(row_count - EDGE, EDGE)]
        + [(j * chunk, chunk) for j in range(chunks - 1)]
        + [((chunks - 1) * chunk, chunk - EDGE)]
    )

    def token_copy(k, q, way):
        rows = pl.ds(*pieces[q])
        source = tokens_any.at[rows, :] if k == 0 else held.at[order[k], rows, :]
        return pltpu.make_async_remote_copy(
            src_ref=source,
            dst_ref=held.at[order[k], rows, :],
            send_sem=tok_send.at[way, k, q],
            recv_sem=tok_recv.at[order[k], q],
            device_id={"tp": t + (inward if way == 0 else -inward)},
            device_id_type=MESH,
        )

    for q in range(len(pieces)):
        token_copy(0, q, 0).start()

        @pl.when(middle)
        def _():
            token_copy(0, q, 1).start()

    for k in range(tp_count):
        weight_load(k).start()
    loads[2].start()
    loads[3].start()

    loads[0].wait()
    own = held[t].astype(jnp.float32)
    sums = jnp.sum(own * own, axis=1, keepdims=True)
    squares[t] = jnp.transpose(jnp.broadcast_to(sums, (row_count, 128)))[:8]

    def square_copy(shift, slot):
        return pltpu.make_async_remote_copy(
            src_ref=squares.at[slot],
            dst_ref=squares.at[slot],
            send_sem=sq_send.at[shift],
            recv_sem=sq_recv.at[slot],
            device_id={"tp": lax.rem(t + shift, tp_count)},
            device_id_type=MESH,
        )

    for shift in range(1, tp_count):
        square_copy(shift, t).start()

    def peer_copy(shift, source, target, send_sem, recv_sem):
        peer = lax.rem(me + shift, part_count)
        return pltpu.make_async_remote_copy(
            src_ref=source.at[peer],
            dst_ref=target.at[me],
            send_sem=send_sem.at[peer],
            recv_sem=recv_sem.at[me],
            device_id={"ctx": peer},
            device_id_type=MESH,
        )

    def send_to_peers(*refs):
        def go(shift, _):
            peer_copy(shift, *refs).start()
            return 0

        lax.fori_loop(1, part_count, go, 0)

    def sent_to_peers(*refs):
        def go(shift, _):
            peer_copy(shift, *refs).wait_send()
            return 0

        lax.fori_loop(1, part_count, go, 0)

    def wait_for_peers(source, target, send_sem, recv_sem):
        def go(shift, _):
            peer = lax.rem(me + shift, part_count)
            pltpu.make_async_remote_copy(
                src_ref=source.at[peer],
                dst_ref=target.at[peer],
                send_sem=send_sem.at[peer],
                recv_sem=recv_sem.at[peer],
                device_id={"ctx": peer},
                device_id_type=MESH,
            ).wait_recv()
            return 0

        lax.fori_loop(1, part_count, go, 0)

    loads[1].wait()
    group = max(128, channels)
    for j in range(width // group):
        columns = pl.ds(j * group, group)
        blocks = group // channels
        f_sent[pl.ds(j * blocks, blocks)] = (
            jnp.transpose(filt[:, columns]).astype(jnp.bfloat16).reshape(blocks, channels, row_count)
        )
    send_to_peers(f_sent, f_got, f_send, f_recv)
    f_got[me] = f_sent[me]

    for shift in range(1, tp_count):
        square_copy(shift, lax.rem(t + shift, tp_count)).wait_recv()
    mean = (squares[0] + squares[1] + squares[2] + squares[3]) * (1.0 / (tp_count * features))
    inverse = lax.rsqrt(mean + 1e-06)
    scale[...] = jnp.transpose(jnp.broadcast_to(inverse[:1], (128, row_count)))

    def normalise(k, start, size):
        rows = pl.ds(start, size)
        values = held[order[k], rows, :].astype(jnp.float32) * scale[rows, :1] * gain_ref[order[k]]
        normed[rows, :] = values.astype(jnp.bfloat16)

    def weights_of(k, i):
        return weight[i, pl.ds(pl.multiple_of(order[k] * features, features), features), :]

    def accumulate(k):
        normalise(k, 0, row_count)
        weight_load(k).wait()

        def one(i, _):
            product = jnp.dot(normed[...], weights_of(k, i), preferred_element_type=jnp.float32)
            total[i] = product if k == 0 else total[i] + product
            return 0

        lax.fori_loop(0, 3, one, 0)

    accumulate(0)

    def outer(parts, lanes, high):
        for k in range(part_count + 1):
            turns = [turn_of(a, k, part_count) for a in range(part_count)]
            cos, sin = cos_ref[pl.ds(k, 1), lanes], sin_ref[pl.ds(k, 1), lanes]
            real = weighted([(c[0], p) for c, p in zip(turns, parts)])
            imag = weighted([(-c[1], p) for c, p in zip(turns, parts)])
            rows = pl.ds(k * channels, channels)
            if imag is None:
                turned[rows, lanes] = (real * cos).astype(jnp.bfloat16)
                turned[rows, high] = (-real * sin).astype(jnp.bfloat16)
            else:
                turned[rows, lanes] = (real * cos + imag * sin).astype(jnp.bfloat16)
                turned[rows, high] = (imag * cos - real * sin).astype(jnp.bfloat16)

    wait_for_peers(f_sent, f_got, f_send, f_recv)
    for j in range(chunks):
        lanes, high = pl.ds(j * chunk, chunk), pl.ds(row_count + j * chunk, chunk)
        outer([f_got[a, :, lanes].astype(jnp.float32) for a in range(part_count)], lanes, high)
    loads[2].wait()
    loads[3].wait()
    unit = 1.0 / (2 * part_count * row_count)
    response[...] = jnp.dot(turned[...], forward[...], preferred_element_type=jnp.float32) * (2.0 * unit)
    for k in (0, part_count):
        rows = pl.ds(k * channels, channels)
        response[rows, :] = response[rows, :] * 0.5

    def arrived(k, q):
        token_copy(k, q, 0).wait_recv()

    for q in range(len(pieces)):
        arrived(1, q)

        @pl.when(middle)
        def _():
            token_copy(1, q, 0).start()
            arrived(2, q)
            token_copy(2, q, 1).start()

    accumulate(1)

    @pl.when(u == 0)
    def _():
        for q in range(len(pieces)):
            arrived(2, q)

    accumulate(2)

    last = tp_count - 1

    def take_piece(q):
        arrived(last, q)

        @pl.when(middle)
        def _():
            token_copy(last, q, 1).start()

    take_piece(0)
    edge = pl.ds(row_count - EDGE, EDGE)
    normalise(last, row_count - EDGE, EDGE)
    weight_load(last).wait()
    for i in range(3):
        product = jnp.dot(normed[edge, :], weights_of(last, i), preferred_element_type=jnp.float32)
        halo_out[i] = (total[i, edge, :] + product).astype(jnp.bfloat16)
    halo = pltpu.make_async_remote_copy(
        src_ref=halo_out,
        dst_ref=halo_in,
        send_sem=halo_sem.at[0],
        recv_sem=halo_sem.at[1],
        device_id={"ctx": lax.rem(me + 1, part_count)},
        device_id_type=MESH,
    )
    halo.start()

    def x_refs(j):
        return x_sent.at[j], x_got.at[j], x_send.at[j], x_recv.at[j]

    def take_signal(j):
        wait_for_peers(*x_refs(j))
        lanes, high = pl.ds(j * chunk, chunk), pl.ds(row_count + j * chunk, chunk)
        outer([x_got[j, a].astype(jnp.float32) for a in range(part_count)], lanes, high)

    for j in range(chunks):
        take_piece(j + 1)
        normalise(last, j * chunk, chunk)
        rows = pl.ds(j * chunk, chunk)
        for i in range(3):
            product = jnp.dot(normed[rows, :], weights_of(last, i), preferred_element_type=jnp.float32)
            projected = (total[i, rows, :] + product).astype(jnp.bfloat16)
            wide[i, pl.ds(8 + j * chunk, chunk), :] = projected.astype(jnp.float32)
        if j == 0:
            halo.wait()
            for i in range(3):
                before = halo_in[i].astype(jnp.float32)[EDGE - 8 :]
                wide[i, pl.ds(0, 8), :] = jnp.where(me > 0, before, jnp.zeros_like(before))

        def branch(i):
            return (
                taps_ref[i, pl.ds(0, 1), :] * wide[i, pl.ds(8 + j * chunk, chunk), :]
                + taps_ref[i, pl.ds(1, 1), :] * wide[i, pl.ds(7 + j * chunk, chunk), :]
                + taps_ref[i, pl.ds(2, 1), :] * wide[i, pl.ds(6 + j * chunk, chunk), :]
            )

        mixed = branch(1) * branch(2)
        x_sent[j] = jnp.transpose(mixed).astype(jnp.bfloat16).reshape(part_count, channels, chunk)
        send_to_peers(*x_refs(j))
        x_got[j, me] = x_sent[j, me]
        direct[rows, :] = skip_ref[...] * mixed
        gate[rows, :] = branch(0)
        if j > 0:
            take_signal(j - 1)
    take_signal(chunks - 1)

    step = row_count // 2
    for n in range(2):
        low, high = pl.ds(n * step, step), pl.ds(row_count + n * step, step)
        real = jnp.dot(turned[...], forward[:, low], preferred_element_type=jnp.float32)
        imag = jnp.dot(turned[...], forward[:, high], preferred_element_type=jnp.float32)
        gain_real, gain_imag = response[:, low], response[:, high]
        spec_turned[:, low] = (real * gain_real - imag * gain_imag).astype(jnp.bfloat16)
        spec_turned[:, high] = (real * gain_imag + imag * gain_real).astype(jnp.bfloat16)

    part = row_count // halves

    def y_refs(h):
        return y_sent.at[h], y_got.at[h], y_send.at[h], y_recv.at[h]

    for h in range(halves):
        back[...] = jnp.dot(spec_turned[...], backward[h], preferred_element_type=jnp.float32)
        lanes = pl.ds(h * part, part)
        low, high = pl.ds(0, part), pl.ds(part, part)
        for k in range(part_count + 1):
            cos, sin = cos_ref[pl.ds(k, 1), lanes], sin_ref[pl.ds(k, 1), lanes]
            rows = pl.ds(k * channels, channels)
            real, imag = back[rows, low], back[rows, high]
            back[rows, low] = real * cos - imag * sin
            if 0 < k < part_count:
                back[rows, high] = real * sin + imag * cos
        for a in range(part_count):
            terms = []
            for k in range(part_count + 1):
                cos, sin = turn_of(a, k, part_count)
                rows = pl.ds(k * channels, channels)
                terms.append((cos, back[rows, low]))
                if sin != 0.0:
                    terms.append((-sin, back[rows, high]))
            y_sent[h, a] = weighted(terms).astype(jnp.bfloat16)
        send_to_peers(*y_refs(h))
        y_got[h, me] = y_sent[h, me]

    for h in range(halves):
        wait_for_peers(*y_refs(h))
        rows = pl.ds(h * part, part)
        convolved = jnp.transpose(y_got[h].astype(jnp.float32).reshape(width, part))
        out_ref[rows, :] = (gate[rows, :] * (convolved + direct[rows, :])).astype(jnp.bfloat16)

    for q in range(len(pieces)):
        token_copy(0, q, 0).wait_send()

        @pl.when(middle)
        def _():
            token_copy(1, q, 0).wait_send()
            for k in (0, 2, 3):
                token_copy(k, q, 1).wait_send()

    for shift in range(1, tp_count):
        square_copy(shift, t).wait_send()
    sent_to_peers(f_sent, f_got, f_send, f_recv)
    for j in range(chunks):
        sent_to_peers(*x_refs(j))
    for h in range(halves):
        sent_to_peers(*y_refs(h))


def body(tokens, norm_gain, proj_weight, short_taps, long_filter, skip_gain):
    part_count, tp_count = lax.axis_size("ctx"), lax.axis_size("tp")
    row_count, width = long_filter.shape
    features = tokens.shape[1]
    channels = width // part_count
    chunk, halves = 128, 2
    chunks, pieces = row_count // chunk, row_count // chunk + 1
    rows = (part_count + 1) * channels
    cos, sin = twist_tables(part_count, row_count)
    forward, backward = inner_tables(row_count, halves)
    held = pl.BlockSpec(memory_space=pltpu.VMEM)
    away = pl.BlockSpec(memory_space=pl.ANY)
    bf16, f32 = jnp.bfloat16, jnp.float32
    dma = pltpu.SemaphoreType.DMA
    part = row_count // halves
    return pl.pallas_call(
        functools.partial(block_kernel, part_count, tp_count, chunk, halves),
        out_shape=jax.ShapeDtypeStruct((row_count, width), bf16),
        in_specs=[away, held, away, held, away, held, held, held, away, away],
        out_specs=held,
        scratch_shapes=[
            pltpu.VMEM((tp_count, row_count, features), bf16),
            pltpu.VMEM(proj_weight.shape, bf16),
            pltpu.VMEM((3, row_count, width), f32),
            pltpu.VMEM((row_count, features), bf16),
            pltpu.VMEM((row_count, 128), f32),
            pltpu.VMEM((tp_count, 8, row_count), f32),
            pltpu.VMEM((row_count, width), f32),
            pltpu.VMEM((part_count, channels, row_count), bf16),
            pltpu.VMEM((part_count, channels, row_count), bf16),
            pltpu.VMEM((rows, 2 * row_count), bf16),
            pltpu.VMEM((rows, 2 * row_count), f32),
            pltpu.VMEM((rows, 2 * row_count), bf16),
            pltpu.VMEM((3, EDGE, width), bf16),
            pltpu.VMEM((3, EDGE, width), bf16),
            pltpu.VMEM((3, row_count + 8, width), f32),
            pltpu.VMEM((row_count, width), f32),
            pltpu.VMEM((row_count, width), f32),
            pltpu.VMEM((chunks, part_count, channels, chunk), bf16),
            pltpu.VMEM((chunks, part_count, channels, chunk), bf16),
            pltpu.VMEM((rows, 2 * part), f32),
            pltpu.VMEM((halves, part_count, channels, part), bf16),
            pltpu.VMEM((halves, part_count, channels, part), bf16),
            pltpu.VMEM(forward.shape, bf16),
            pltpu.VMEM(backward.shape, bf16),
            dma((4,)),
            dma((tp_count,)),
            dma((2, tp_count, pieces)),
            dma((tp_count, pieces)),
            dma((tp_count,)),
            dma((tp_count,)),
            dma((part_count,)),
            dma((part_count,)),
            dma((2,)),
            dma((chunks, part_count)),
            dma((chunks, part_count)),
            dma((halves, part_count)),
            dma((halves, part_count)),
        ],
        compiler_params=pltpu.CompilerParams(
            vmem_limit_bytes=60 << 20, collective_id=0, has_side_effects=True
        ),
        name="hyena_block",
    )(
        tokens, norm_gain.reshape(tp_count, 1, features), proj_weight, short_taps, long_filter,
        skip_gain[None, :], cos, sin, forward, backward,
    )


def solution(mesh):
    placed = (
        P("ctx", "tp"),
        P(),
        P(None, None, "tp"),
        P(None, None, "tp"),
        P("ctx", "tp"),
        P("tp"),
    )
    return jax.shard_map(
        body, mesh=mesh, in_specs=placed, out_specs=P("ctx", "tp"), check_vma=False
    )
```

```python
import functools
import math

import jax
import jax.numpy as jnp
import numpy as np
from jax import lax
from jax.experimental import pallas as pl
from jax.experimental.pallas import tpu as pltpu
from jax.sharding import PartitionSpec as P

MESH = pl.DeviceIdType.MESH
EDGE = 16


def twist_tables(part_count, row_count):
    turn = np.arange(part_count + 1)[:, None] * np.arange(row_count)[None, :]
    angles = turn * (math.pi / (part_count * row_count))
    return np.cos(angles).astype(np.float32), np.sin(angles).astype(np.float32)


def inner_tables(row_count, halves):
    turn = np.arange(row_count)[:, None] * np.arange(row_count)[None, :] % row_count
    angles = turn * (2.0 * math.pi / row_count)
    cos, sin = np.cos(angles), np.sin(angles)
    forward = np.block([[cos, -sin], [sin, cos]])
    backward = np.block([[cos, sin], [-sin, cos]])
    part = row_count // halves
    backward = np.stack(
        [
            np.concatenate(
                [
                    backward[:, h * part : (h + 1) * part],
                    backward[:, row_count + h * part : row_count + (h + 1) * part],
                ],
                axis=1,
            )
            for h in range(halves)
        ]
    )
    return forward.astype(jnp.bfloat16), backward.astype(jnp.bfloat16)


def turn_of(a, k, part_count):
    step = a * k % (2 * part_count)
    cos = math.cos(math.pi * step / part_count)
    sin = math.sin(math.pi * step / part_count)
    return (0.0 if abs(cos) < 1e-12 else cos, 0.0 if abs(sin) < 1e-12 else sin)


def weighted(terms):
    total = None
    for factor, term in terms:
        if factor == 0.0:
            continue
        scaled = term if abs(factor - 1.0) < 1e-12 else -term if abs(factor + 1.0) < 1e-12 else factor * term
        total = scaled if total is None else total + scaled
    return total


def block_kernel(
    part_count, tp_count, chunk, halves,
    tokens_any, gain_ref, weight_any, taps_ref, filter_any, skip_ref, cos_ref, sin_ref, forward_any, backward_any,
    out_ref,
    held, weight, total, normed, scale, squares, filt, f_sent, f_got, turned, response, spec_turned,
    halo_out, halo_in, wide, direct, x_sent, x_got, back, y_sent, y_got, forward, backward, lent, p_sent, p_got,
    load_sem, weight_sem, tok_send, tok_recv, sq_send, sq_recv, f_send, f_recv, halo_sem, x_send, x_recv, y_send, y_recv,
    w_send, w_recv, wp_send, wp_recv, wc_send, wc_recv, p_send, p_recv,
):
    row_count, width = out_ref.shape
    features = held.shape[2]
    channels = width // part_count
    chunks = row_count // chunk
    share = features // part_count
    mates = part_count // 2
    me = lax.axis_index("ctx")
    t = lax.axis_index("tp")
    place, core = me // 2, lax.rem(me, 2)
    upper = t // (tp_count // 2)
    u = t + upper * (tp_count - 1 - 2 * t)
    inward = 1 - 2 * upper
    middle = u == 1
    end = u == 0

    def mirrored(o):
        return o + upper * (tp_count - 1 - 2 * o)

    order = [t, mirrored(1 - u), mirrored(2), mirrored(3)]
    slots = (2, 2, 0, 1)
    first, gated = (1, 2), 0

    loads = [
        pltpu.make_async_copy(source, target, load_sem.at[i])
        for i, (source, target) in enumerate(
            [
                (tokens_any, held.at[t]),
                (filter_any, filt),
                (forward_any, forward),
                (backward_any, backward),
            ]
        )
    ]

    def block(k):
        return pl.ds(pl.multiple_of(order[k] * features, features), features)

    def weight_load(k):
        return pltpu.make_async_copy(weight_any.at[:, block(k), :], weight.at[:, block(k), :], weight_sem.at[k])

    barrier = pltpu.get_barrier_semaphore()

    def greet_ctx(shift, _):
        pl.semaphore_signal(barrier, inc=1, device_id={"ctx": lax.rem(me + shift, part_count)}, device_id_type=MESH)
        return 0

    lax.fori_loop(1, part_count, greet_ctx, 0)
    for shift in range(1, tp_count):
        pl.semaphore_signal(barrier, inc=1, device_id={"tp": lax.rem(t + shift, tp_count)}, device_id_type=MESH)
    loads[0].start()
    loads[1].start()
    pl.semaphore_wait(barrier, part_count - 1 + tp_count - 1)

    pieces = (
        [(row_count - EDGE, EDGE)]
        + [(j * chunk, chunk) for j in range(chunks - 1)]
        + [((chunks - 1) * chunk, chunk - EDGE)]
    )
    every = range(len(pieces))
    plain = (0, 1)

    def token_copy(k, q, way):
        rows = pl.ds(*pieces[q])
        source = tokens_any.at[rows, :] if k == 0 else held.at[order[k], rows, :]
        return pltpu.make_async_remote_copy(
            src_ref=source,
            dst_ref=held.at[order[k], rows, :],
            send_sem=tok_send.at[way, k, q],
            recv_sem=tok_recv.at[order[k], q],
            device_id={"tp": t + (inward if way == 0 else -inward)},
            device_id_type=MESH,
        )

    def weight_copy(i, b, local):
        rows = pl.ds(pl.multiple_of(order[2 + b] * features + me * share, share), share)
        target = lent.at[i, b, place, core]
        return pltpu.make_async_remote_copy(
            src_ref=target if local else weight_any.at[i, rows, :],
            dst_ref=target,
            send_sem=w_send.at[i, b],
            recv_sem=w_recv.at[i, b],
            device_id={"tp": t + inward},
            device_id_type=MESH,
        )

    def mate_copy(i, shift, slot):
        return pltpu.make_async_remote_copy(
            src_ref=lent.at[i, :, slot, core],
            dst_ref=lent.at[i, :, slot, core],
            send_sem=wp_send.at[i, shift],
            recv_sem=wp_recv.at[i, slot],
            device_id={"ctx": lax.rem(me + 2 * shift, part_count)},
            device_id_type=MESH,
        )

    def twin_copy(i, side):
        return pltpu.make_async_remote_copy(
            src_ref=lent.at[i, :, :, side],
            dst_ref=lent.at[i, :, :, side],
            send_sem=wc_send.at[i],
            recv_sem=wc_recv.at[i],
            device_id={"ctx": me + 1 - 2 * core},
            device_id_type=MESH,
        )

    def partial_copy(i, r, way):
        return pltpu.make_async_remote_copy(
            src_ref=p_sent.at[r - 1, i],
            dst_ref=p_got.at[r - 1, i],
            send_sem=p_send.at[r - 1, i],
            recv_sem=p_recv.at[r - 1, i],
            device_id={"tp": t + way * inward},
            device_id_type=MESH,
        )

    @pl.when(end)
    def _():
        for b in range(2):
            weight_copy(first[0], b, False).start()

    @pl.when(middle)
    def _():
        for q in plain:
            token_copy(0, q, 0).start()
            token_copy(0, q, 1).start()

    loads[0].wait()
    own = held[t].astype(jnp.float32)
    sums = jnp.sum(own * own, axis=1, keepdims=True)
    squares[t] = jnp.transpose(jnp.broadcast_to(sums, (row_count, 128)))[:8]

    def square_copy(shift, slot):
        return pltpu.make_async_remote_copy(
            src_ref=squares.at[slot],
            dst_ref=squares.at[slot],
            send_sem=sq_send.at[shift],
            recv_sem=sq_recv.at[slot],
            device_id={"tp": lax.rem(t + shift, tp_count)},
            device_id_type=MESH,
        )

    for shift in range(1, tp_count):
        square_copy(shift, t).start()

    @pl.when(end)
    def _():
        for i in (first[1], gated):
            for b in range(2):
                weight_copy(i, b, False).start()
        for q in every:
            token_copy(0, q, 0).start()

    @pl.when(middle)
    def _():
        for q in every:
            if q not in plain:
                token_copy(0, q, 0).start()
                token_copy(0, q, 1).start()

    for k in range(tp_count):
        weight_load(k).start()
    loads[2].start()
    loads[3].start()

    def peer_copy(shift, source, target, send_sem, recv_sem):
        peer = lax.rem(me + shift, part_count)
        return pltpu.make_async_remote_copy(
            src_ref=source.at[peer],
            dst_ref=target.at[me],
            send_sem=send_sem.at[peer],
            recv_sem=recv_sem.at[me],
            device_id={"ctx": peer},
            device_id_type=MESH,
        )

    def send_to_peers(*refs):
        def go(shift, _):
            peer_copy(shift, *refs).start()
            return 0

        lax.fori_loop(1, part_count, go, 0)

    def sent_to_peers(*refs):
        def go(shift, _):
            peer_copy(shift, *refs).wait_send()
            return 0

        lax.fori_loop(1, part_count, go, 0)

    def wait_for_peers(source, target, send_sem, recv_sem):
        def go(shift, _):
            peer = lax.rem(me + shift, part_count)
            pltpu.make_async_remote_copy(
                src_ref=source.at[peer],
                dst_ref=target.at[peer],
                send_sem=send_sem.at[peer],
                recv_sem=recv_sem.at[peer],
                device_id={"ctx": peer},
                device_id_type=MESH,
            ).wait_recv()
            return 0

        lax.fori_loop(1, part_count, go, 0)

    loads[1].wait()
    group = max(128, channels)
    for j in range(width // group):
        columns = pl.ds(j * group, group)
        blocks = group // channels
        f_sent[pl.ds(j * blocks, blocks)] = (
            jnp.transpose(filt[:, columns]).astype(jnp.bfloat16).reshape(blocks, channels, row_count)
        )
    send_to_peers(f_sent, f_got, f_send, f_recv)
    f_got[me] = f_sent[me]

    def row_scales():
        for shift in range(1, tp_count):
            square_copy(shift, lax.rem(t + shift, tp_count)).wait_recv()
        mean = (squares[0] + squares[1] + squares[2] + squares[3]) * (1.0 / (tp_count * features))
        inverse = lax.rsqrt(mean + 1e-06)
        scale[...] = jnp.transpose(jnp.broadcast_to(inverse[:1], (128, row_count)))

    def normalise(k, start, size):
        rows = pl.ds(start, size)
        values = held[order[k], rows, :].astype(jnp.float32) * scale[rows, :1] * gain_ref[order[k]]
        normed[slots[k], rows, :] = values.astype(jnp.bfloat16)

    def product(k, i, rows):
        return jnp.dot(normed[slots[k], rows, :], weight[i, block(k), :], preferred_element_type=jnp.float32)

    def accumulate(k):
        def one(i, _):
            added = product(k, i, slice(None))
            total[i] = added if k == 0 else total[i] + added
            return 0

        weight_load(k).wait()
        lax.fori_loop(0, 3, one, 0)

    def outer(parts, lanes, high):
        for k in range(part_count + 1):
            turns = [turn_of(a, k, part_count) for a in range(part_count)]
            cos, sin = cos_ref[pl.ds(k, 1), lanes], sin_ref[pl.ds(k, 1), lanes]
            real = weighted([(c[0], p) for c, p in zip(turns, parts)])
            imag = weighted([(-c[1], p) for c, p in zip(turns, parts)])
            rows = pl.ds(k * channels, channels)
            if imag is None:
                turned[rows, lanes] = (real * cos).astype(jnp.bfloat16)
                turned[rows, high] = (-real * sin).astype(jnp.bfloat16)
            else:
                turned[rows, lanes] = (real * cos + imag * sin).astype(jnp.bfloat16)
                turned[rows, high] = (imag * cos - real * sin).astype(jnp.bfloat16)

    def filter_spectrum():
        wait_for_peers(f_sent, f_got, f_send, f_recv)
        for j in range(chunks):
            lanes, high = pl.ds(j * chunk, chunk), pl.ds(row_count + j * chunk, chunk)
            outer([f_got[a, :, lanes].astype(jnp.float32) for a in range(part_count)], lanes, high)
        loads[2].wait()
        loads[3].wait()
        unit = 1.0 / (2 * part_count * row_count)
        response[...] = jnp.dot(turned[...], forward[...], preferred_element_type=jnp.float32) * (2.0 * unit)
        for k in (0, part_count):
            rows = pl.ds(k * channels, channels)
            response[rows, :] = response[rows, :] * 0.5

    def arrived(k, q):
        token_copy(k, q, 0).wait_recv()

    edge = pl.ds(row_count - EDGE, EDGE)

    @pl.when(middle)
    def _():
        def share_out(i):
            for b in range(2):
                weight_copy(i, b, True).wait_recv()

            def go(shift, _):
                mate_copy(i, shift, place).start()
                return 0

            lax.fori_loop(1, mates, go, 0)

        def to_twin(i):
            def go(shift, _):
                mate_copy(i, shift, lax.rem(place + shift, mates)).wait_recv()
                return 0

            lax.fori_loop(1, mates, go, 0)
            twin_copy(i, core).start()

        def partial(i, r):
            rows = pl.ds(r * chunk, chunk)
            value = None
            for b in range(2):
                matrix = lent[i, b].reshape(features, width)
                part = jnp.dot(normed[b, rows, :], matrix, preferred_element_type=jnp.float32)
                value = part if value is None else value + part
            p_sent[r - 1, i] = value.astype(jnp.bfloat16)
            partial_copy(i, r, -1).start()

        def inward_piece(q):
            arrived(1, q)
            token_copy(1, q, 0).start()

        share_out(first[0])
        for q in plain:
            arrived(2, q)
            token_copy(2, q, 1).start()
        share_out(first[1])
        row_scales()
        normalise(0, 0, row_count)
        accumulate(0)
        share_out(gated)
        filter_spectrum()
        for q in plain:
            inward_piece(q)
        to_twin(first[0])
        for q in every:
            if q not in plain:
                arrived(2, q)
        normalise(2, 0, row_count)
        accumulate(2)
        for q in plain:
            arrived(3, q)
            token_copy(3, q, 1).start()
        normalise(3, 0, chunk)
        inward_piece(2)
        to_twin(first[1])
        twin_copy(first[0], 1 - core).wait_recv()
        for r in range(1, chunks):
            arrived(3, r + 1)
            normalise(3, r * chunk, chunk)
            if r == 1:
                twin_copy(first[1], 1 - core).wait_recv()
            for i in first:
                partial(i, r)
            if r + 2 < len(pieces):
                inward_piece(r + 2)
        normalise(1, 0, row_count)
        accumulate(1)
        to_twin(gated)
        accumulate(3)
        for i in range(3):
            halo_out[i] = total[i, edge, :].astype(jnp.bfloat16)
        twin_copy(gated, 1 - core).wait_recv()
        for r in range(1, chunks):
            partial(gated, r)

    @pl.when(end)
    def _():
        row_scales()
        normalise(0, 0, row_count)
        accumulate(0)
        filter_spectrum()
        for q in every:
            arrived(1, q)
        normalise(1, 0, row_count)
        accumulate(1)
        for k in (2, 3):
            weight_load(k).wait()
            arrived(k, 0)
            normalise(k, row_count - EDGE, EDGE)
        for i in range(3):
            halo_out[i] = (total[i, edge, :] + product(2, i, edge) + product(3, i, edge)).astype(jnp.bfloat16)

    halo = pltpu.make_async_remote_copy(
        src_ref=halo_out,
        dst_ref=halo_in,
        send_sem=halo_sem.at[0],
        recv_sem=halo_sem.at[1],
        device_id={"ctx": lax.rem(me + 1, part_count)},
        device_id_type=MESH,
    )
    halo.start()

    @pl.when(end)
    def _():
        for k in (2, 3):
            arrived(k, 1)
            normalise(k, 0, chunk)
        rows = pl.ds(0, chunk)
        for i in range(3):
            total[i, rows, :] = total[i, rows, :] + product(2, i, rows) + product(3, i, rows)

    halo.wait()
    for i in range(3):
        before = halo_in[i].astype(jnp.float32)[EDGE - 8 :]
        wide[i, pl.ds(0, 8), :] = jnp.where(me > 0, before, jnp.zeros_like(before))

    def add_partial(i, j):
        rows = pl.ds(j * chunk, chunk)
        if j > 0:

            @pl.when(end)
            def _():
                partial_copy(i, j, 1).wait_recv()
                total[i, rows, :] = total[i, rows, :] + p_got[j - 1, i].astype(jnp.float32)

        projected = total[i, rows, :].astype(jnp.bfloat16)
        wide[i, pl.ds(8 + j * chunk, chunk), :] = projected.astype(jnp.float32)

    def branch(i, start, size):
        return (
            taps_ref[i, pl.ds(0, 1), :] * wide[i, pl.ds(8 + start, size), :]
            + taps_ref[i, pl.ds(1, 1), :] * wide[i, pl.ds(7 + start, size), :]
            + taps_ref[i, pl.ds(2, 1), :] * wide[i, pl.ds(6 + start, size), :]
        )

    def x_refs(j):
        return x_sent.at[j], x_got.at[j], x_send.at[j], x_recv.at[j]

    def take_signal(j):
        wait_for_peers(*x_refs(j))
        lanes, high = pl.ds(j * chunk, chunk), pl.ds(row_count + j * chunk, chunk)
        outer([x_got[j, a].astype(jnp.float32) for a in range(part_count)], lanes, high)

    for j in range(chunks):
        for i in first:
            add_partial(i, j)
        mixed = branch(1, j * chunk, chunk) * branch(2, j * chunk, chunk)
        x_sent[j] = jnp.transpose(mixed).astype(jnp.bfloat16).reshape(part_count, channels, chunk)
        send_to_peers(*x_refs(j))
        x_got[j, me] = x_sent[j, me]
        direct[pl.ds(j * chunk, chunk), :] = skip_ref[...] * mixed
        if j > 0:
            take_signal(j - 1)
    take_signal(chunks - 1)

    step = row_count // 2
    for n in range(2):
        low, high = pl.ds(n * step, step), pl.ds(row_count + n * step, step)
        real = jnp.dot(turned[...], forward[:, low], preferred_element_type=jnp.float32)
        imag = jnp.dot(turned[...], forward[:, high], preferred_element_type=jnp.float32)
        gain_real, gain_imag = response[:, low], response[:, high]
        spec_turned[:, low] = (real * gain_real - imag * gain_imag).astype(jnp.bfloat16)
        spec_turned[:, high] = (real * gain_imag + imag * gain_real).astype(jnp.bfloat16)

    part = row_count // halves

    def y_refs(h):
        return y_sent.at[h], y_got.at[h], y_send.at[h], y_recv.at[h]

    for h in range(halves):
        back[...] = jnp.dot(spec_turned[...], backward[h], preferred_element_type=jnp.float32)
        lanes = pl.ds(h * part, part)
        low, high = pl.ds(0, part), pl.ds(part, part)
        for k in range(part_count + 1):
            cos, sin = cos_ref[pl.ds(k, 1), lanes], sin_ref[pl.ds(k, 1), lanes]
            rows = pl.ds(k * channels, channels)
            real, imag = back[rows, low], back[rows, high]
            back[rows, low] = real * cos - imag * sin
            if 0 < k < part_count:
                back[rows, high] = real * sin + imag * cos
        for a in range(part_count):
            terms = []
            for k in range(part_count + 1):
                cos, sin = turn_of(a, k, part_count)
                rows = pl.ds(k * channels, channels)
                terms.append((cos, back[rows, low]))
                if sin != 0.0:
                    terms.append((-sin, back[rows, high]))
            y_sent[h, a] = weighted(terms).astype(jnp.bfloat16)
        send_to_peers(*y_refs(h))
        y_got[h, me] = y_sent[h, me]

    for j in range(chunks):
        add_partial(gated, j)

    for h in range(halves):
        gate = branch(gated, h * part, part)
        wait_for_peers(*y_refs(h))
        rows = pl.ds(h * part, part)
        convolved = jnp.transpose(y_got[h].astype(jnp.float32).reshape(width, part))
        out_ref[rows, :] = (gate * (convolved + direct[rows, :])).astype(jnp.bfloat16)

    @pl.when(end)
    def _():
        for i in range(3):
            for b in range(2):
                weight_copy(i, b, False).wait_send()
        for q in every:
            token_copy(0, q, 0).wait_send()

    @pl.when(middle)
    def _():
        for q in every:
            token_copy(0, q, 0).wait_send()
            token_copy(0, q, 1).wait_send()
            token_copy(1, q, 0).wait_send()
        for q in plain:
            token_copy(2, q, 1).wait_send()
            token_copy(3, q, 1).wait_send()
        for i in range(3):

            def go(shift, _):
                mate_copy(i, shift, place).wait_send()
                return 0

            lax.fori_loop(1, mates, go, 0)
            twin_copy(i, core).wait_send()
            for r in range(1, chunks):
                partial_copy(i, r, -1).wait_send()

    for shift in range(1, tp_count):
        square_copy(shift, t).wait_send()
    sent_to_peers(f_sent, f_got, f_send, f_recv)
    for j in range(chunks):
        sent_to_peers(*x_refs(j))
    for h in range(halves):
        sent_to_peers(*y_refs(h))


def body(tokens, norm_gain, proj_weight, short_taps, long_filter, skip_gain):
    part_count, tp_count = lax.axis_size("ctx"), lax.axis_size("tp")
    row_count, width = long_filter.shape
    features = tokens.shape[1]
    channels = width // part_count
    chunk, halves = 128, 2
    chunks, pieces = row_count // chunk, row_count // chunk + 1
    rows = (part_count + 1) * channels
    cos, sin = twist_tables(part_count, row_count)
    forward, backward = inner_tables(row_count, halves)
    held = pl.BlockSpec(memory_space=pltpu.VMEM)
    away = pl.BlockSpec(memory_space=pl.ANY)
    bf16, f32 = jnp.bfloat16, jnp.float32
    dma = pltpu.SemaphoreType.DMA
    part = row_count // halves
    return pl.pallas_call(
        functools.partial(block_kernel, part_count, tp_count, chunk, halves),
        out_shape=jax.ShapeDtypeStruct((row_count, width), bf16),
        in_specs=[away, held, away, held, away, held, held, held, away, away],
        out_specs=held,
        scratch_shapes=[
            pltpu.VMEM((tp_count, row_count, features), bf16),
            pltpu.VMEM(proj_weight.shape, bf16),
            pltpu.VMEM((3, row_count, width), f32),
            pltpu.VMEM((3, row_count, features), bf16),
            pltpu.VMEM((row_count, 128), f32),
            pltpu.VMEM((tp_count, 8, row_count), f32),
            pltpu.VMEM((row_count, width), f32),
            pltpu.VMEM((part_count, channels, row_count), bf16),
            pltpu.VMEM((part_count, channels, row_count), bf16),
            pltpu.VMEM((rows, 2 * row_count), bf16),
            pltpu.VMEM((rows, 2 * row_count), f32),
            pltpu.VMEM((rows, 2 * row_count), bf16),
            pltpu.VMEM((3, EDGE, width), bf16),
            pltpu.VMEM((3, EDGE, width), bf16),
            pltpu.VMEM((3, row_count + 8, width), f32),
            pltpu.VMEM((row_count, width), f32),
            pltpu.VMEM((chunks, part_count, channels, chunk), bf16),
            pltpu.VMEM((chunks, part_count, channels, chunk), bf16),
            pltpu.VMEM((rows, 2 * part), f32),
            pltpu.VMEM((halves, part_count, channels, part), bf16),
            pltpu.VMEM((halves, part_count, channels, part), bf16),
            pltpu.VMEM(forward.shape, bf16),
            pltpu.VMEM(backward.shape, bf16),
            pltpu.VMEM((3, 2, part_count // 2, 2, features // part_count, width), bf16),
            pltpu.VMEM((chunks - 1, 3, chunk, width), bf16),
            pltpu.VMEM((chunks - 1, 3, chunk, width), bf16),
            dma((4,)),
            dma((tp_count,)),
            dma((2, tp_count, pieces)),
            dma((tp_count, pieces)),
            dma((tp_count,)),
            dma((tp_count,)),
            dma((part_count,)),
            dma((part_count,)),
            dma((2,)),
            dma((chunks, part_count)),
            dma((chunks, part_count)),
            dma((halves, part_count)),
            dma((halves, part_count)),
            dma((3, 2)),
            dma((3, 2)),
            dma((3, part_count // 2)),
            dma((3, part_count // 2)),
            dma((3,)),
            dma((3,)),
            dma((chunks - 1, 3)),
            dma((chunks - 1, 3)),
        ],
        compiler_params=pltpu.CompilerParams(
            vmem_limit_bytes=60 << 20, collective_id=0, has_side_effects=True
        ),
        name="hyena_block",
    )(
        tokens, norm_gain.reshape(tp_count, 1, features), proj_weight, short_taps, long_filter,
        skip_gain[None, :], cos, sin, forward, backward,
    )


def solution(mesh):
    placed = (
        P("ctx", "tp"),
        P(),
        P(None, None, "tp"),
        P(None, None, "tp"),
        P("ctx", "tp"),
        P("tp"),
    )
    return jax.shard_map(
        body, mesh=mesh, in_specs=placed, out_specs=P("ctx", "tp"), check_vma=False
    )
```

```python
import functools
import math

import jax
import jax.numpy as jnp
import numpy as np
from jax import lax
from jax.experimental import pallas as pl
from jax.experimental.pallas import tpu as pltpu
from jax.sharding import PartitionSpec as P

MESH = pl.DeviceIdType.MESH
EDGE = 16


def twist_tables(part_count, row_count):
    turn = np.arange(part_count + 1)[:, None] * np.arange(row_count)[None, :]
    angles = turn * (math.pi / (part_count * row_count))
    return np.cos(angles).astype(np.float32), np.sin(angles).astype(np.float32)


def inner_tables(row_count, halves):
    turn = np.arange(row_count)[:, None] * np.arange(row_count)[None, :] % row_count
    angles = turn * (2.0 * math.pi / row_count)
    cos, sin = np.cos(angles), np.sin(angles)
    forward = np.block([[cos, -sin], [sin, cos]])
    backward = np.block([[cos, sin], [-sin, cos]])
    part = row_count // halves
    backward = np.stack(
        [
            np.concatenate(
                [
                    backward[:, h * part : (h + 1) * part],
                    backward[:, row_count + h * part : row_count + (h + 1) * part],
                ],
                axis=1,
            )
            for h in range(halves)
        ]
    )
    return forward.astype(jnp.bfloat16), backward.astype(jnp.bfloat16)


def turn_of(a, k, part_count):
    step = a * k % (2 * part_count)
    cos = math.cos(math.pi * step / part_count)
    sin = math.sin(math.pi * step / part_count)
    return (0.0 if abs(cos) < 1e-12 else cos, 0.0 if abs(sin) < 1e-12 else sin)


def weighted(terms):
    total = None
    for factor, term in terms:
        if factor == 0.0:
            continue
        scaled = term if abs(factor - 1.0) < 1e-12 else -term if abs(factor + 1.0) < 1e-12 else factor * term
        total = scaled if total is None else total + scaled
    return total


def block_kernel(
    part_count, tp_count, chunk, halves,
    tokens_any, gain_ref, weight_any, taps_ref, filter_any, skip_ref, cos_ref, sin_ref, forward_any, backward_any,
    out_ref,
    held, weight, total, normed, scale, squares, filt, f_sent, f_got, turned, response, spec_turned,
    halo_out, halo_in, wide, direct, x_sent, x_got, back, y_sent, y_got, forward, backward, lent, p_sent, p_got,
    load_sem, weight_sem, tok_send, tok_recv, sq_send, sq_recv, f_send, f_recv, halo_sem, x_send, x_recv, y_send, y_recv,
    w_send, w_recv, wp_send, wp_recv, wc_send, wc_recv, p_send, p_recv,
):
    row_count, width = out_ref.shape
    features = held.shape[2]
    channels = width // part_count
    chunks = row_count // chunk
    share = features // part_count
    mates = part_count // 2
    me = lax.axis_index("ctx")
    t = lax.axis_index("tp")
    place, core = me // 2, lax.rem(me, 2)
    upper = t // (tp_count // 2)
    u = t + upper * (tp_count - 1 - 2 * t)
    inward = 1 - 2 * upper
    middle = u == 1
    end = u == 0

    def mirrored(o):
        return o + upper * (tp_count - 1 - 2 * o)

    order = [t, mirrored(1 - u), mirrored(2), mirrored(3)]
    slots = (2, 2, 0, 1)
    first, gated = (1, 2), 0

    loads = [
        pltpu.make_async_copy(source, target, load_sem.at[i])
        for i, (source, target) in enumerate(
            [
                (tokens_any, held.at[t]),
                (filter_any, filt),
                (forward_any, forward),
                (backward_any, backward),
            ]
        )
    ]

    def block(k):
        return pl.ds(pl.multiple_of(order[k] * features, features), features)

    def weight_load(k):
        return pltpu.make_async_copy(weight_any.at[:, block(k), :], weight.at[:, block(k), :], weight_sem.at[k])

    barrier = pltpu.get_barrier_semaphore()

    def greet_ctx(shift, _):
        pl.semaphore_signal(barrier, inc=1, device_id={"ctx": lax.rem(me + shift, part_count)}, device_id_type=MESH)
        return 0

    lax.fori_loop(1, part_count, greet_ctx, 0)
    for shift in range(1, tp_count):
        pl.semaphore_signal(barrier, inc=1, device_id={"tp": lax.rem(t + shift, tp_count)}, device_id_type=MESH)
    loads[0].start()
    loads[1].start()
    pl.semaphore_wait(barrier, part_count - 1 + tp_count - 1)

    pieces = (
        [(row_count - EDGE, EDGE)]
        + [(j * chunk, chunk) for j in range(chunks - 1)]
        + [((chunks - 1) * chunk, chunk - EDGE)]
    )
    every = range(len(pieces))
    plain = (0, 1)

    def token_copy(k, q, way):
        rows = pl.ds(*pieces[q])
        source = tokens_any.at[rows, :] if k == 0 else held.at[order[k], rows, :]
        return pltpu.make_async_remote_copy(
            src_ref=source,
            dst_ref=held.at[order[k], rows, :],
            send_sem=tok_send.at[way, k, q],
            recv_sem=tok_recv.at[order[k], q],
            device_id={"tp": t + (inward if way == 0 else -inward)},
            device_id_type=MESH,
        )

    def weight_copy(i, b, local):
        rows = pl.ds(pl.multiple_of(order[2 + b] * features + me * share, share), share)
        target = lent.at[i, b, place, core]
        return pltpu.make_async_remote_copy(
            src_ref=target if local else weight_any.at[i, rows, :],
            dst_ref=target,
            send_sem=w_send.at[i, b],
            recv_sem=w_recv.at[i, b],
            device_id={"tp": t + inward},
            device_id_type=MESH,
        )

    def mate_copy(i, shift, slot):
        return pltpu.make_async_remote_copy(
            src_ref=lent.at[i, :, slot, core],
            dst_ref=lent.at[i, :, slot, core],
            send_sem=wp_send.at[i, shift],
            recv_sem=wp_recv.at[i, slot],
            device_id={"ctx": lax.rem(me + 2 * shift, part_count)},
            device_id_type=MESH,
        )

    def twin_copy(i, side):
        return pltpu.make_async_remote_copy(
            src_ref=lent.at[i, :, :, side],
            dst_ref=lent.at[i, :, :, side],
            send_sem=wc_send.at[i],
            recv_sem=wc_recv.at[i],
            device_id={"ctx": me + 1 - 2 * core},
            device_id_type=MESH,
        )

    def partial_copy(i, r, way):
        return pltpu.make_async_remote_copy(
            src_ref=p_sent.at[r - 1, i],
            dst_ref=p_got.at[r - 1, i],
            send_sem=p_send.at[r - 1, i],
            recv_sem=p_recv.at[r - 1, i],
            device_id={"tp": t + way * inward},
            device_id_type=MESH,
        )

    @pl.when(end)
    def _():
        for b in range(2):
            weight_copy(first[0], b, False).start()

    @pl.when(middle)
    def _():
        for q in plain:
            token_copy(0, q, 0).start()
            token_copy(0, q, 1).start()

    loads[0].wait()
    own = held[t].astype(jnp.float32)
    sums = jnp.sum(own * own, axis=1, keepdims=True)
    squares[t] = jnp.transpose(jnp.broadcast_to(sums, (row_count, 128)))[:8]

    def square_copy(shift, slot):
        return pltpu.make_async_remote_copy(
            src_ref=squares.at[slot],
            dst_ref=squares.at[slot],
            send_sem=sq_send.at[shift],
            recv_sem=sq_recv.at[slot],
            device_id={"tp": lax.rem(t + shift, tp_count)},
            device_id_type=MESH,
        )

    for shift in range(1, tp_count):
        square_copy(shift, t).start()

    @pl.when(end)
    def _():
        for b in range(2):
            weight_copy(first[1], b, False).start()
        for q in every:
            if q == 3:
                for b in range(2):
                    weight_copy(gated, b, False).start()
            token_copy(0, q, 0).start()

    @pl.when(middle)
    def _():
        for q in every:
            if q not in plain:
                token_copy(0, q, 0).start()
                token_copy(0, q, 1).start()

    for k in range(tp_count):
        weight_load(k).start()
    loads[2].start()
    loads[3].start()

    def peer_copy(shift, source, target, send_sem, recv_sem):
        peer = lax.rem(me + shift, part_count)
        return pltpu.make_async_remote_copy(
            src_ref=source.at[peer],
            dst_ref=target.at[me],
            send_sem=send_sem.at[peer],
            recv_sem=recv_sem.at[me],
            device_id={"ctx": peer},
            device_id_type=MESH,
        )

    def send_to_peers(*refs):
        def go(shift, _):
            peer_copy(shift, *refs).start()
            return 0

        lax.fori_loop(1, part_count, go, 0)

    def sent_to_peers(*refs):
        def go(shift, _):
            peer_copy(shift, *refs).wait_send()
            return 0

        lax.fori_loop(1, part_count, go, 0)

    def wait_for_peers(source, target, send_sem, recv_sem):
        def go(shift, _):
            peer = lax.rem(me + shift, part_count)
            pltpu.make_async_remote_copy(
                src_ref=source.at[peer],
                dst_ref=target.at[peer],
                send_sem=send_sem.at[peer],
                recv_sem=recv_sem.at[peer],
                device_id={"ctx": peer},
                device_id_type=MESH,
            ).wait_recv()
            return 0

        lax.fori_loop(1, part_count, go, 0)

    loads[1].wait()
    group = max(128, channels)
    for j in range(width // group):
        columns = pl.ds(j * group, group)
        blocks = group // channels
        f_sent[pl.ds(j * blocks, blocks)] = (
            jnp.transpose(filt[:, columns]).astype(jnp.bfloat16).reshape(blocks, channels, row_count)
        )
    send_to_peers(f_sent, f_got, f_send, f_recv)
    f_got[me] = f_sent[me]

    def row_scales():
        for shift in range(1, tp_count):
            square_copy(shift, lax.rem(t + shift, tp_count)).wait_recv()
        mean = (squares[0] + squares[1] + squares[2] + squares[3]) * (1.0 / (tp_count * features))
        inverse = lax.rsqrt(mean + 1e-06)
        scale[...] = jnp.transpose(jnp.broadcast_to(inverse[:1], (128, row_count)))

    def normalise(k, start, size):
        rows = pl.ds(start, size)
        values = held[order[k], rows, :].astype(jnp.float32) * scale[rows, :1] * gain_ref[order[k]]
        normed[slots[k], rows, :] = values.astype(jnp.bfloat16)

    def product(k, i, rows):
        return jnp.dot(normed[slots[k], rows, :], weight[i, block(k), :], preferred_element_type=jnp.float32)

    def accumulate(k):
        def one(i, _):
            added = product(k, i, slice(None))
            total[i] = added if k == 0 else total[i] + added
            return 0

        weight_load(k).wait()
        lax.fori_loop(0, 3, one, 0)

    def outer(parts, lanes, high):
        for k in range(part_count + 1):
            turns = [turn_of(a, k, part_count) for a in range(part_count)]
            cos, sin = cos_ref[pl.ds(k, 1), lanes], sin_ref[pl.ds(k, 1), lanes]
            real = weighted([(c[0], p) for c, p in zip(turns, parts)])
            imag = weighted([(-c[1], p) for c, p in zip(turns, parts)])
            rows = pl.ds(k * channels, channels)
            if imag is None:
                turned[rows, lanes] = (real * cos).astype(jnp.bfloat16)
                turned[rows, high] = (-real * sin).astype(jnp.bfloat16)
            else:
                turned[rows, lanes] = (real * cos + imag * sin).astype(jnp.bfloat16)
                turned[rows, high] = (imag * cos - real * sin).astype(jnp.bfloat16)

    def filter_spectrum():
        wait_for_peers(f_sent, f_got, f_send, f_recv)

        def one(j, _):
            lanes = pl.ds(pl.multiple_of(j * chunk, chunk), chunk)
            high = pl.ds(pl.multiple_of(row_count + j * chunk, chunk), chunk)
            outer([f_got[a, :, lanes].astype(jnp.float32) for a in range(part_count)], lanes, high)
            return 0

        lax.fori_loop(0, chunks, one, 0)
        loads[2].wait()
        loads[3].wait()
        unit = 1.0 / (2 * part_count * row_count)
        response[...] = jnp.dot(turned[...], forward[...], preferred_element_type=jnp.float32) * (2.0 * unit)
        for k in (0, part_count):
            rows = pl.ds(k * channels, channels)
            response[rows, :] = response[rows, :] * 0.5

    def arrived(k, q):
        token_copy(k, q, 0).wait_recv()

    edge = pl.ds(row_count - EDGE, EDGE)
    halo = pltpu.make_async_remote_copy(
        src_ref=halo_out,
        dst_ref=halo_in,
        send_sem=halo_sem.at[0],
        recv_sem=halo_sem.at[1],
        device_id={"ctx": lax.rem(me + 1, part_count)},
        device_id_type=MESH,
    )

    def take_halo():
        halo.wait()
        for i in range(3):
            before = halo_in[i].astype(jnp.float32)[EDGE - 8 :]
            wide[i, pl.ds(0, 8), :] = jnp.where(me > 0, before, jnp.zeros_like(before))

    def widen(i, j):
        projected = total[i, pl.ds(j * chunk, chunk), :].astype(jnp.bfloat16)
        wide[i, pl.ds(8 + j * chunk, chunk), :] = projected.astype(jnp.float32)

    def branch(i, start, size):
        return (
            taps_ref[i, pl.ds(0, 1), :] * wide[i, pl.ds(8 + start, size), :]
            + taps_ref[i, pl.ds(1, 1), :] * wide[i, pl.ds(7 + start, size), :]
            + taps_ref[i, pl.ds(2, 1), :] * wide[i, pl.ds(6 + start, size), :]
        )

    def x_refs(j):
        return x_sent.at[j], x_got.at[j], x_send.at[j], x_recv.at[j]

    def send_signal(j):
        mixed = branch(1, j * chunk, chunk) * branch(2, j * chunk, chunk)
        x_sent[j] = jnp.transpose(mixed).astype(jnp.bfloat16).reshape(part_count, channels, chunk)
        send_to_peers(*x_refs(j))
        x_got[j, me] = x_sent[j, me]
        direct[pl.ds(j * chunk, chunk), :] = skip_ref[...] * mixed

    def take_signal(j):
        wait_for_peers(*x_refs(j))
        lanes, high = pl.ds(j * chunk, chunk), pl.ds(row_count + j * chunk, chunk)
        outer([x_got[j, a].astype(jnp.float32) for a in range(part_count)], lanes, high)

    @pl.when(middle)
    def _():
        def share_out(i):
            for b in range(2):
                weight_copy(i, b, True).wait_recv()

            def go(shift, _):
                mate_copy(i, shift, place).start()
                return 0

            lax.fori_loop(1, mates, go, 0)

        def to_twin(i):
            def go(shift, _):
                mate_copy(i, shift, lax.rem(place + shift, mates)).wait_recv()
                return 0

            lax.fori_loop(1, mates, go, 0)
            twin_copy(i, core).start()

        def partial(i, r):
            rows = pl.ds(r * chunk, chunk)
            value = None
            for b in range(2):
                matrix = lent[i, b].reshape(features, width)
                part = jnp.dot(normed[b, rows, :], matrix, preferred_element_type=jnp.float32)
                value = part if value is None else value + part
            p_sent[r - 1, i] = value.astype(jnp.bfloat16)
            partial_copy(i, r, -1).start()

        def inward_piece(q):
            arrived(1, q)
            token_copy(1, q, 0).start()

        def add_far(i, rows):
            total[i, rows, :] = total[i, rows, :] + product(3, i, rows)

        share_out(first[0])
        for q in plain:
            arrived(2, q)
            token_copy(2, q, 1).start()
        share_out(first[1])
        row_scales()
        normalise(0, 0, row_count)
        accumulate(0)
        for q in plain:
            inward_piece(q)
        filter_spectrum()
        to_twin(first[0])
        inward_piece(2)
        for q in every:
            if q not in plain:
                arrived(2, q)
        normalise(2, 0, row_count)
        accumulate(2)
        share_out(gated)
        for q in plain:
            arrived(3, q)
            token_copy(3, q, 1).start()
        normalise(3, 0, chunk)
        to_twin(first[1])
        inward_piece(3)
        twin_copy(first[0], 1 - core).wait_recv()
        weight_load(3).wait()
        for r in range(1, chunks):
            arrived(3, r + 1)
            normalise(3, r * chunk, chunk)
            if r == 1:
                twin_copy(first[1], 1 - core).wait_recv()
            for i in first:
                partial(i, r)
            if r == chunks - 2:
                inward_piece(len(pieces) - 1)
                normalise(1, 0, row_count)
                accumulate(1)
                for i in first:
                    add_far(i, pl.ds(0, row_count - chunk))
                    for j in range(chunks - 1):
                        widen(i, j)
                to_twin(gated)
                for j in range(1, chunks - 1):
                    send_signal(j)
        last = pl.ds(row_count - chunk, chunk)
        for i in range(3):
            add_far(i, last)
            halo_out[i] = total[i, edge, :].astype(jnp.bfloat16)
        halo.start()
        for i in first:
            widen(i, chunks - 1)
        send_signal(chunks - 1)
        take_halo()
        send_signal(0)
        add_far(gated, pl.ds(0, row_count - chunk))
        twin_copy(gated, 1 - core).wait_recv()
        for r in range(1, chunks):
            partial(gated, r)
        for j in range(1, chunks):
            take_signal(j)
        take_signal(0)

    @pl.when(end)
    def _():
        row_scales()
        normalise(0, 0, row_count)
        accumulate(0)
        filter_spectrum()
        for q in every:
            arrived(1, q)
        normalise(1, 0, row_count)
        accumulate(1)
        for k in (2, 3):
            weight_load(k).wait()
            arrived(k, 0)
            normalise(k, row_count - EDGE, EDGE)
        for i in range(3):
            halo_out[i] = (total[i, edge, :] + product(2, i, edge) + product(3, i, edge)).astype(jnp.bfloat16)
        halo.start()
        for k in (2, 3):
            arrived(k, 1)
            normalise(k, 0, chunk)
        rows = pl.ds(0, chunk)
        for i in range(3):
            total[i, rows, :] = total[i, rows, :] + product(2, i, rows) + product(3, i, rows)
        take_halo()
        for j in range(chunks):
            for i in first:
                if j > 0:
                    rows = pl.ds(j * chunk, chunk)
                    partial_copy(i, j, 1).wait_recv()
                    total[i, rows, :] = total[i, rows, :] + p_got[j - 1, i].astype(jnp.float32)
                widen(i, j)
            send_signal(j)
            if j > 0:
                take_signal(j - 1)
        take_signal(chunks - 1)

    step = row_count // 2
    for n in range(2):
        low, high = pl.ds(n * step, step), pl.ds(row_count + n * step, step)
        real = jnp.dot(turned[...], forward[:, low], preferred_element_type=jnp.float32)
        imag = jnp.dot(turned[...], forward[:, high], preferred_element_type=jnp.float32)
        gain_real, gain_imag = response[:, low], response[:, high]
        spec_turned[:, low] = (real * gain_real - imag * gain_imag).astype(jnp.bfloat16)
        spec_turned[:, high] = (real * gain_imag + imag * gain_real).astype(jnp.bfloat16)

    part = row_count // halves

    def y_refs(h):
        return y_sent.at[h], y_got.at[h], y_send.at[h], y_recv.at[h]

    for h in range(halves):
        back[...] = jnp.dot(spec_turned[...], backward[h], preferred_element_type=jnp.float32)
        lanes = pl.ds(h * part, part)
        low, high = pl.ds(0, part), pl.ds(part, part)
        for k in range(part_count + 1):
            cos, sin = cos_ref[pl.ds(k, 1), lanes], sin_ref[pl.ds(k, 1), lanes]
            rows = pl.ds(k * channels, channels)
            real, imag = back[rows, low], back[rows, high]
            back[rows, low] = real * cos - imag * sin
            if 0 < k < part_count:
                back[rows, high] = real * sin + imag * cos
        for a in range(part_count):
            terms = []
            for k in range(part_count + 1):
                cos, sin = turn_of(a, k, part_count)
                rows = pl.ds(k * channels, channels)
                terms.append((cos, back[rows, low]))
                if sin != 0.0:
                    terms.append((-sin, back[rows, high]))
            y_sent[h, a] = weighted(terms).astype(jnp.bfloat16)
        send_to_peers(*y_refs(h))
        y_got[h, me] = y_sent[h, me]

    @pl.when(end)
    def _():
        for j in range(1, chunks):
            rows = pl.ds(j * chunk, chunk)
            partial_copy(gated, j, 1).wait_recv()
            total[gated, rows, :] = total[gated, rows, :] + p_got[j - 1, gated].astype(jnp.float32)

    for j in range(chunks):
        widen(gated, j)

    for h in range(halves):
        gate = branch(gated, h * part, part)
        wait_for_peers(*y_refs(h))
        rows = pl.ds(h * part, part)
        convolved = jnp.transpose(y_got[h].astype(jnp.float32).reshape(width, part))
        out_ref[rows, :] = (gate * (convolved + direct[rows, :])).astype(jnp.bfloat16)

    @pl.when(end)
    def _():
        for i in range(3):
            for b in range(2):
                weight_copy(i, b, False).wait_send()
        for q in every:
            token_copy(0, q, 0).wait_send()

    @pl.when(middle)
    def _():
        for q in every:
            token_copy(0, q, 0).wait_send()
            token_copy(0, q, 1).wait_send()
            token_copy(1, q, 0).wait_send()
        for q in plain:
            token_copy(2, q, 1).wait_send()
            token_copy(3, q, 1).wait_send()
        for i in range(3):

            def go(shift, _):
                mate_copy(i, shift, place).wait_send()
                return 0

            lax.fori_loop(1, mates, go, 0)
            twin_copy(i, core).wait_send()
            for r in range(1, chunks):
                partial_copy(i, r, -1).wait_send()

    for shift in range(1, tp_count):
        square_copy(shift, t).wait_send()
    sent_to_peers(f_sent, f_got, f_send, f_recv)
    for j in range(chunks):
        sent_to_peers(*x_refs(j))
    for h in range(halves):
        sent_to_peers(*y_refs(h))


def body(tokens, norm_gain, proj_weight, short_taps, long_filter, skip_gain):
    part_count, tp_count = lax.axis_size("ctx"), lax.axis_size("tp")
    row_count, width = long_filter.shape
    features = tokens.shape[1]
    channels = width // part_count
    chunk, halves = 128, 2
    chunks, pieces = row_count // chunk, row_count // chunk + 1
    rows = (part_count + 1) * channels
    cos, sin = twist_tables(part_count, row_count)
    forward, backward = inner_tables(row_count, halves)
    held = pl.BlockSpec(memory_space=pltpu.VMEM)
    away = pl.BlockSpec(memory_space=pl.ANY)
    bf16, f32 = jnp.bfloat16, jnp.float32
    dma = pltpu.SemaphoreType.DMA
    part = row_count // halves
    return pl.pallas_call(
        functools.partial(block_kernel, part_count, tp_count, chunk, halves),
        out_shape=jax.ShapeDtypeStruct((row_count, width), bf16),
        in_specs=[away, held, away, held, away, held, held, held, away, away],
        out_specs=held,
        scratch_shapes=[
            pltpu.VMEM((tp_count, row_count, features), bf16),
            pltpu.VMEM(proj_weight.shape, bf16),
            pltpu.VMEM((3, row_count, width), f32),
            pltpu.VMEM((3, row_count, features), bf16),
            pltpu.VMEM((row_count, 128), f32),
            pltpu.VMEM((tp_count, 8, row_count), f32),
            pltpu.VMEM((row_count, width), f32),
            pltpu.VMEM((part_count, channels, row_count), bf16),
            pltpu.VMEM((part_count, channels, row_count), bf16),
            pltpu.VMEM((rows, 2 * row_count), bf16),
            pltpu.VMEM((rows, 2 * row_count), f32),
            pltpu.VMEM((rows, 2 * row_count), bf16),
            pltpu.VMEM((3, EDGE, width), bf16),
            pltpu.VMEM((3, EDGE, width), bf16),
            pltpu.VMEM((3, row_count + 8, width), f32),
            pltpu.VMEM((row_count, width), f32),
            pltpu.VMEM((chunks, part_count, channels, chunk), bf16),
            pltpu.VMEM((chunks, part_count, channels, chunk), bf16),
            pltpu.VMEM((rows, 2 * part), f32),
            pltpu.VMEM((halves, part_count, channels, part), bf16),
            pltpu.VMEM((halves, part_count, channels, part), bf16),
            pltpu.VMEM(forward.shape, bf16),
            pltpu.VMEM(backward.shape, bf16),
            pltpu.VMEM((3, 2, part_count // 2, 2, features // part_count, width), bf16),
            pltpu.VMEM((chunks - 1, 3, chunk, width), bf16),
            pltpu.VMEM((chunks - 1, 3, chunk, width), bf16),
            dma((4,)),
            dma((tp_count,)),
            dma((2, tp_count, pieces)),
            dma((tp_count, pieces)),
            dma((tp_count,)),
            dma((tp_count,)),
            dma((part_count,)),
            dma((part_count,)),
            dma((2,)),
            dma((chunks, part_count)),
            dma((chunks, part_count)),
            dma((halves, part_count)),
            dma((halves, part_count)),
            dma((3, 2)),
            dma((3, 2)),
            dma((3, part_count // 2)),
            dma((3, part_count // 2)),
            dma((3,)),
            dma((3,)),
            dma((chunks - 1, 3)),
            dma((chunks - 1, 3)),
        ],
        compiler_params=pltpu.CompilerParams(
            vmem_limit_bytes=60 << 20, collective_id=0, has_side_effects=True
        ),
        name="hyena_block",
    )(
        tokens, norm_gain.reshape(tp_count, 1, features), proj_weight, short_taps, long_filter,
        skip_gain[None, :], cos, sin, forward, backward,
    )


def solution(mesh):
    placed = (
        P("ctx", "tp"),
        P(),
        P(None, None, "tp"),
        P(None, None, "tp"),
        P("ctx", "tp"),
        P("tp"),
    )
    return jax.shard_map(
        body, mesh=mesh, in_specs=placed, out_specs=P("ctx", "tp"), check_vma=False
    )
```

```python
import functools
import math

import jax
import jax.numpy as jnp
import numpy as np
from jax import lax
from jax.experimental import pallas as pl
from jax.experimental.pallas import tpu as pltpu
from jax.sharding import PartitionSpec as P

MESH = pl.DeviceIdType.MESH
EDGE = 16


def twist_tables(part_count, row_count):
    turn = np.arange(part_count + 1)[:, None] * np.arange(row_count)[None, :]
    angles = turn * (math.pi / (part_count * row_count))
    return np.cos(angles).astype(np.float32), np.sin(angles).astype(np.float32)


def inner_tables(row_count, halves):
    turn = np.arange(row_count)[:, None] * np.arange(row_count)[None, :] % row_count
    angles = turn * (2.0 * math.pi / row_count)
    cos, sin = np.cos(angles), np.sin(angles)
    forward = np.block([[cos, -sin], [sin, cos]])
    backward = np.block([[cos, sin], [-sin, cos]])
    part = row_count // halves
    backward = np.stack(
        [
            np.concatenate(
                [
                    backward[:, h * part : (h + 1) * part],
                    backward[:, row_count + h * part : row_count + (h + 1) * part],
                ],
                axis=1,
            )
            for h in range(halves)
        ]
    )
    return forward.astype(jnp.bfloat16), backward.astype(jnp.bfloat16)


def turn_of(a, k, part_count):
    step = a * k % (2 * part_count)
    cos = math.cos(math.pi * step / part_count)
    sin = math.sin(math.pi * step / part_count)
    return (0.0 if abs(cos) < 1e-12 else cos, 0.0 if abs(sin) < 1e-12 else sin)


def weighted(terms):
    total = None
    for factor, term in terms:
        if factor == 0.0:
            continue
        scaled = term if abs(factor - 1.0) < 1e-12 else -term if abs(factor + 1.0) < 1e-12 else factor * term
        total = scaled if total is None else total + scaled
    return total


def block_kernel(
    part_count, tp_count, chunk, halves, groups,
    tokens_any, gain_ref, weight_any, taps_ref, filter_any, skip_ref, cos_ref, sin_ref, forward_any, backward_any,
    out_ref,
    held, weight, total, normed, scale, squares, filt, f_sent, f_got, turned, response, spec_turned,
    halo_out, halo_in, wide, direct, x_sent, x_got, back, y_sent, y_got, forward, backward, lent, p_sent, p_got,
    load_sem, weight_sem, tok_send, tok_recv, sq_send, sq_recv, f_send, f_recv, halo_sem, x_send, x_recv, y_send, y_recv,
    w_send, w_recv, wp_send, wp_recv, wc_send, wc_recv, p_send, p_recv,
):
    row_count, width = out_ref.shape
    features = held.shape[2]
    channels = width // part_count
    each = channels // groups
    span = (part_count + 1) * each
    chunks = row_count // chunk
    share = features // part_count
    mates = part_count // 2
    me = lax.axis_index("ctx")
    t = lax.axis_index("tp")
    place, core = me // 2, lax.rem(me, 2)
    upper = t // (tp_count // 2)
    u = t + upper * (tp_count - 1 - 2 * t)
    inward = 1 - 2 * upper
    middle = u == 1
    end = u == 0

    def mirrored(o):
        return o + upper * (tp_count - 1 - 2 * o)

    order = [t, mirrored(1 - u), mirrored(2), mirrored(3)]
    slots = (2, 2, 0, 1)
    first, gated = (1, 2), 0

    loads = [
        pltpu.make_async_copy(source, target, load_sem.at[i])
        for i, (source, target) in enumerate(
            [
                (tokens_any, held.at[t]),
                (filter_any, filt),
                (forward_any, forward),
                (backward_any, backward),
            ]
        )
    ]

    def block(k):
        return pl.ds(pl.multiple_of(order[k] * features, features), features)

    def weight_load(k):
        return pltpu.make_async_copy(weight_any.at[:, block(k), :], weight.at[:, block(k), :], weight_sem.at[k])

    barrier = pltpu.get_barrier_semaphore()

    def greet_ctx(shift, _):
        pl.semaphore_signal(barrier, inc=1, device_id={"ctx": lax.rem(me + shift, part_count)}, device_id_type=MESH)
        return 0

    lax.fori_loop(1, part_count, greet_ctx, 0)
    for shift in range(1, tp_count):
        pl.semaphore_signal(barrier, inc=1, device_id={"tp": lax.rem(t + shift, tp_count)}, device_id_type=MESH)
    loads[0].start()
    loads[1].start()
    pl.semaphore_wait(barrier, part_count - 1 + tp_count - 1)

    pieces = (
        [(row_count - EDGE, EDGE)]
        + [(j * chunk, chunk) for j in range(chunks - 1)]
        + [((chunks - 1) * chunk, chunk - EDGE)]
    )
    every = range(len(pieces))
    plain = (0, 1)

    def token_copy(k, q, way):
        rows = pl.ds(*pieces[q])
        source = tokens_any.at[rows, :] if k == 0 else held.at[order[k], rows, :]
        return pltpu.make_async_remote_copy(
            src_ref=source,
            dst_ref=held.at[order[k], rows, :],
            send_sem=tok_send.at[way, k, q],
            recv_sem=tok_recv.at[order[k], q],
            device_id={"tp": t + (inward if way == 0 else -inward)},
            device_id_type=MESH,
        )

    def weight_copy(i, b, local):
        rows = pl.ds(pl.multiple_of(order[2 + b] * features + me * share, share), share)
        target = lent.at[i, b, place, core]
        return pltpu.make_async_remote_copy(
            src_ref=target if local else weight_any.at[i, rows, :],
            dst_ref=target,
            send_sem=w_send.at[i, b],
            recv_sem=w_recv.at[i, b],
            device_id={"tp": t + inward},
            device_id_type=MESH,
        )

    def mate_copy(i, shift, slot):
        return pltpu.make_async_remote_copy(
            src_ref=lent.at[i, :, slot, core],
            dst_ref=lent.at[i, :, slot, core],
            send_sem=wp_send.at[i, shift],
            recv_sem=wp_recv.at[i, slot],
            device_id={"ctx": lax.rem(me + 2 * shift, part_count)},
            device_id_type=MESH,
        )

    def twin_copy(i, side):
        return pltpu.make_async_remote_copy(
            src_ref=lent.at[i, :, :, side],
            dst_ref=lent.at[i, :, :, side],
            send_sem=wc_send.at[i],
            recv_sem=wc_recv.at[i],
            device_id={"ctx": me + 1 - 2 * core},
            device_id_type=MESH,
        )

    def partial_copy(i, r, way):
        return pltpu.make_async_remote_copy(
            src_ref=p_sent.at[r - 1, i],
            dst_ref=p_got.at[r - 1, i],
            send_sem=p_send.at[r - 1, i],
            recv_sem=p_recv.at[r - 1, i],
            device_id={"tp": t + way * inward},
            device_id_type=MESH,
        )

    @pl.when(end)
    def _():
        for b in range(2):
            weight_copy(first[0], b, False).start()

    @pl.when(middle)
    def _():
        for q in plain:
            token_copy(0, q, 0).start()
            token_copy(0, q, 1).start()

    loads[0].wait()
    own = held[t].astype(jnp.float32)
    sums = jnp.sum(own * own, axis=1, keepdims=True)
    squares[t] = jnp.transpose(jnp.broadcast_to(sums, (row_count, 128)))[:8]

    def square_copy(shift, slot):
        return pltpu.make_async_remote_copy(
            src_ref=squares.at[slot],
            dst_ref=squares.at[slot],
            send_sem=sq_send.at[shift],
            recv_sem=sq_recv.at[slot],
            device_id={"tp": lax.rem(t + shift, tp_count)},
            device_id_type=MESH,
        )

    for shift in range(1, tp_count):
        square_copy(shift, t).start()

    @pl.when(end)
    def _():
        for b in range(2):
            weight_copy(first[1], b, False).start()
        for q in every:
            if q == 4:
                for b in range(2):
                    weight_copy(gated, b, False).start()
            token_copy(0, q, 0).start()

    @pl.when(middle)
    def _():
        for q in every:
            if q not in plain:
                token_copy(0, q, 1).start()
                token_copy(0, q, 0).start()

    for k in range(tp_count):
        weight_load(k).start()
    loads[2].start()
    loads[3].start()

    def peer_copy(shift, source, target, send_sem, recv_sem):
        peer = lax.rem(me + shift, part_count)
        return pltpu.make_async_remote_copy(
            src_ref=source.at[peer],
            dst_ref=target.at[me],
            send_sem=send_sem.at[peer],
            recv_sem=recv_sem.at[me],
            device_id={"ctx": peer},
            device_id_type=MESH,
        )

    def send_to_peers(*refs):
        def go(shift, _):
            peer_copy(shift, *refs).start()
            return 0

        lax.fori_loop(1, part_count, go, 0)

    def sent_to_peers(*refs):
        def go(shift, _):
            peer_copy(shift, *refs).wait_send()
            return 0

        lax.fori_loop(1, part_count, go, 0)

    def wait_for_peers(source, target, send_sem, recv_sem):
        def go(shift, _):
            peer = lax.rem(me + shift, part_count)
            pltpu.make_async_remote_copy(
                src_ref=source.at[peer],
                dst_ref=target.at[peer],
                send_sem=send_sem.at[peer],
                recv_sem=recv_sem.at[peer],
                device_id={"ctx": peer},
                device_id_type=MESH,
            ).wait_recv()
            return 0

        lax.fori_loop(1, part_count, go, 0)

    loads[1].wait()
    group = max(128, channels)
    for j in range(width // group):
        columns = pl.ds(j * group, group)
        blocks = group // channels
        f_sent[pl.ds(j * blocks, blocks)] = (
            jnp.transpose(filt[:, columns]).astype(jnp.bfloat16).reshape(blocks, channels, row_count)
        )
    f_got[me] = f_sent[me]
    send_to_peers(f_sent, f_got, f_send, f_recv)

    def row_scales():
        for shift in range(1, tp_count):
            square_copy(shift, lax.rem(t + shift, tp_count)).wait_recv()
        mean = (squares[0] + squares[1] + squares[2] + squares[3]) * (1.0 / (tp_count * features))
        inverse = lax.rsqrt(mean + 1e-06)
        scale[...] = jnp.transpose(jnp.broadcast_to(inverse[:1], (128, row_count)))

    def normalise(k, start, size):
        rows = pl.ds(start, size)
        values = held[order[k], rows, :].astype(jnp.float32) * scale[rows, :1] * gain_ref[order[k]]
        normed[slots[k], rows, :] = values.astype(jnp.bfloat16)

    def product(k, i, rows):
        return jnp.dot(normed[slots[k], rows, :], weight[i, block(k), :], preferred_element_type=jnp.float32)

    def accumulate(k):
        def one(i, _):
            added = product(k, i, slice(None))
            total[i] = added if k == 0 else total[i] + added
            return 0

        weight_load(k).wait()
        lax.fori_loop(0, 3, one, 0)

    def outer(parts, lanes, high):
        for k in range(part_count + 1):
            turns = [turn_of(a, k, part_count) for a in range(part_count)]
            cos, sin = cos_ref[pl.ds(k, 1), lanes], sin_ref[pl.ds(k, 1), lanes]
            real = weighted([(c[0], p) for c, p in zip(turns, parts)])
            imag = weighted([(-c[1], p) for c, p in zip(turns, parts)])
            if imag is None:
                low_value, high_value = real * cos, -real * sin
            else:
                low_value, high_value = real * cos + imag * sin, imag * cos - real * sin
            for g in range(groups):
                rows = pl.ds(g * span + k * each, each)
                turned[rows, lanes] = low_value[g * each : (g + 1) * each].astype(jnp.bfloat16)
                turned[rows, high] = high_value[g * each : (g + 1) * each].astype(jnp.bfloat16)

    def filter_spectrum():
        wait_for_peers(f_sent, f_got, f_send, f_recv)

        def one(j, _):
            lanes = pl.ds(pl.multiple_of(j * chunk, chunk), chunk)
            high = pl.ds(pl.multiple_of(row_count + j * chunk, chunk), chunk)
            outer([f_got[a, :, lanes].astype(jnp.float32) for a in range(part_count)], lanes, high)
            return 0

        lax.fori_loop(0, chunks, one, 0)
        loads[2].wait()
        loads[3].wait()
        unit = 1.0 / (2 * part_count * row_count)
        response[...] = jnp.dot(turned[...], forward[...], preferred_element_type=jnp.float32) * (2.0 * unit)
        for g in range(groups):
            for k in (0, part_count):
                rows = pl.ds(g * span + k * each, each)
                response[rows, :] = response[rows, :] * 0.5

    def arrived(k, q):
        token_copy(k, q, 0).wait_recv()

    edge = pl.ds(row_count - EDGE, EDGE)
    halo = pltpu.make_async_remote_copy(
        src_ref=halo_out,
        dst_ref=halo_in,
        send_sem=halo_sem.at[0],
        recv_sem=halo_sem.at[1],
        device_id={"ctx": lax.rem(me + 1, part_count)},
        device_id_type=MESH,
    )

    def take_halo():
        halo.wait()
        for i in range(3):
            before = halo_in[i].astype(jnp.float32)[EDGE - 8 :]
            wide[i, pl.ds(0, 8), :] = jnp.where(me > 0, before, jnp.zeros_like(before))

    def widen(i, j):
        projected = total[i, pl.ds(j * chunk, chunk), :].astype(jnp.bfloat16)
        wide[i, pl.ds(8 + j * chunk, chunk), :] = projected.astype(jnp.float32)

    def branch(i, start, size):
        return (
            taps_ref[i, pl.ds(0, 1), :] * wide[i, pl.ds(8 + start, size), :]
            + taps_ref[i, pl.ds(1, 1), :] * wide[i, pl.ds(7 + start, size), :]
            + taps_ref[i, pl.ds(2, 1), :] * wide[i, pl.ds(6 + start, size), :]
        )

    def x_refs(j):
        return x_sent.at[j], x_got.at[j], x_send.at[j], x_recv.at[j]

    def send_signal(j):
        mixed = branch(1, j * chunk, chunk) * branch(2, j * chunk, chunk)
        x_sent[j] = jnp.transpose(mixed).astype(jnp.bfloat16).reshape(part_count, channels, chunk)
        send_to_peers(*x_refs(j))
        x_got[j, me] = x_sent[j, me]
        direct[pl.ds(j * chunk, chunk), :] = skip_ref[...] * mixed

    def take_signal(j):
        wait_for_peers(*x_refs(j))
        lanes, high = pl.ds(j * chunk, chunk), pl.ds(row_count + j * chunk, chunk)
        outer([x_got[j, a].astype(jnp.float32) for a in range(part_count)], lanes, high)

    @pl.when(middle)
    def _():
        def share_out(i):
            for b in range(2):
                weight_copy(i, b, True).wait_recv()

            def go(shift, _):
                mate_copy(i, shift, place).start()
                return 0

            lax.fori_loop(1, mates, go, 0)

        def to_twin(i):
            def go(shift, _):
                mate_copy(i, shift, lax.rem(place + shift, mates)).wait_recv()
                return 0

            lax.fori_loop(1, mates, go, 0)
            twin_copy(i, core).start()

        def partial(i, r):
            rows = pl.ds(r * chunk, chunk)
            value = None
            for b in range(2):
                matrix = lent[i, b].reshape(features, width)
                part = jnp.dot(normed[b, rows, :], matrix, preferred_element_type=jnp.float32)
                value = part if value is None else value + part
            p_sent[r - 1, i] = value.astype(jnp.bfloat16)
            partial_copy(i, r, -1).start()

        def inward_piece(q):
            arrived(1, q)
            token_copy(1, q, 0).start()

        def add_far(i, rows):
            total[i, rows, :] = total[i, rows, :] + product(3, i, rows)

        share_out(first[0])
        for q in plain:
            arrived(2, q)
            token_copy(2, q, 1).start()
        share_out(first[1])
        row_scales()
        normalise(0, 0, row_count)
        accumulate(0)
        for q in plain:
            inward_piece(q)
        filter_spectrum()
        to_twin(first[0])
        inward_piece(2)
        for q in plain:
            arrived(3, q)
            token_copy(3, q, 1).start()
        normalise(3, 0, chunk)
        for q in range(2, len(pieces) - 1):
            arrived(2, q)
        normalise(2, 0, row_count - chunk)
        inward_piece(3)
        to_twin(first[1])
        twin_copy(first[0], 1 - core).wait_recv()
        weight_load(3).wait()
        for r in range(1, chunks):
            arrived(3, r + 1)
            normalise(3, r * chunk, chunk)
            if r == 1:
                twin_copy(first[1], 1 - core).wait_recv()
            for i in first:
                partial(i, r)
            if r == 1:
                share_out(gated)
                arrived(2, len(pieces) - 1)
                normalise(2, row_count - chunk, chunk)
                accumulate(2)
            if r == chunks - 2:
                inward_piece(len(pieces) - 1)
                normalise(1, 0, row_count)
                accumulate(1)
                for i in first:
                    add_far(i, pl.ds(0, row_count - chunk))
                    for j in range(chunks - 1):
                        widen(i, j)
        for j in range(1, chunks - 1):
            send_signal(j)
        last = pl.ds(row_count - chunk, chunk)
        for i in range(3):
            add_far(i, last)
            halo_out[i] = total[i, edge, :].astype(jnp.bfloat16)
        halo.start()
        for i in first:
            widen(i, chunks - 1)
        send_signal(chunks - 1)
        to_twin(gated)
        take_halo()
        send_signal(0)
        add_far(gated, pl.ds(0, row_count - chunk))
        twin_copy(gated, 1 - core).wait_recv()
        for r in range(1, chunks):
            partial(gated, r)
        for j in range(1, chunks):
            take_signal(j)
        take_signal(0)

    @pl.when(end)
    def _():
        row_scales()
        normalise(0, 0, row_count)
        accumulate(0)
        filter_spectrum()
        for q in every:
            arrived(1, q)
        normalise(1, 0, row_count)
        accumulate(1)
        for k in (2, 3):
            weight_load(k).wait()
            arrived(k, 0)
            normalise(k, row_count - EDGE, EDGE)
        for i in range(3):
            halo_out[i] = (total[i, edge, :] + product(2, i, edge) + product(3, i, edge)).astype(jnp.bfloat16)
        halo.start()
        for k in (2, 3):
            arrived(k, 1)
            normalise(k, 0, chunk)
        rows = pl.ds(0, chunk)
        for i in range(3):
            total[i, rows, :] = total[i, rows, :] + product(2, i, rows) + product(3, i, rows)
        take_halo()
        for j in range(chunks):
            for i in first:
                if j > 0:
                    rows = pl.ds(j * chunk, chunk)
                    partial_copy(i, j, 1).wait_recv()
                    total[i, rows, :] = total[i, rows, :] + p_got[j - 1, i].astype(jnp.float32)
                widen(i, j)
            send_signal(j)
            if j > 0:
                take_signal(j - 1)
        take_signal(chunks - 1)

    part = row_count // halves

    def y_copy(h, g, shift):
        peer = lax.rem(me + shift, part_count)
        return pltpu.make_async_remote_copy(
            src_ref=y_sent.at[h, peer, g],
            dst_ref=y_got.at[h, me, g],
            send_sem=y_send.at[h, g, peer],
            recv_sem=y_recv.at[h, g, me],
            device_id={"ctx": peer},
            device_id_type=MESH,
        )

    def y_start(h, g):
        def go(shift, _):
            y_copy(h, g, shift).start()
            return 0

        lax.fori_loop(1, part_count, go, 0)

    def y_sent_all(h, g):
        def go(shift, _):
            y_copy(h, g, shift).wait_send()
            return 0

        lax.fori_loop(1, part_count, go, 0)

    def y_wait(h, g):
        def go(shift, _):
            peer = lax.rem(me + shift, part_count)
            pltpu.make_async_remote_copy(
                src_ref=y_sent.at[h, peer, g],
                dst_ref=y_got.at[h, peer, g],
                send_sem=y_send.at[h, g, peer],
                recv_sem=y_recv.at[h, g, peer],
                device_id={"ctx": peer},
                device_id_type=MESH,
            ).wait_recv()
            return 0

        lax.fori_loop(1, part_count, go, 0)

    step = row_count // 2
    for g in range(groups):
        mine = pl.ds(g * span, span)
        for n in range(2):
            low, high = pl.ds(n * step, step), pl.ds(row_count + n * step, step)
            real = jnp.dot(turned[mine, :], forward[:, low], preferred_element_type=jnp.float32)
            imag = jnp.dot(turned[mine, :], forward[:, high], preferred_element_type=jnp.float32)
            gain_real, gain_imag = response[mine, low], response[mine, high]
            spec_turned[mine, low] = (real * gain_real - imag * gain_imag).astype(jnp.bfloat16)
            spec_turned[mine, high] = (real * gain_imag + imag * gain_real).astype(jnp.bfloat16)
        for h in range(halves):
            back[h] = jnp.dot(spec_turned[mine, :], backward[h], preferred_element_type=jnp.float32)
            lanes = pl.ds(h * part, part)
            low, high = pl.ds(0, part), pl.ds(part, part)
            for k in range(part_count + 1):
                cos, sin = cos_ref[pl.ds(k, 1), lanes], sin_ref[pl.ds(k, 1), lanes]
                rows = pl.ds(k * each, each)
                real, imag = back[h, rows, low], back[h, rows, high]
                back[h, rows, low] = real * cos - imag * sin
                if 0 < k < part_count:
                    back[h, rows, high] = real * sin + imag * cos
            for a in range(part_count):
                terms = []
                for k in range(part_count + 1):
                    cos, sin = turn_of(a, k, part_count)
                    rows = pl.ds(k * each, each)
                    terms.append((cos, back[h, rows, low]))
                    if sin != 0.0:
                        terms.append((-sin, back[h, rows, high]))
                y_sent[h, a, g] = weighted(terms).astype(jnp.bfloat16)
            y_start(h, g)
            y_got[h, me, g] = y_sent[h, me, g]

    @pl.when(end)
    def _():
        for j in range(1, chunks):
            rows = pl.ds(j * chunk, chunk)
            partial_copy(gated, j, 1).wait_recv()
            total[gated, rows, :] = total[gated, rows, :] + p_got[j - 1, gated].astype(jnp.float32)

    for j in range(chunks):
        widen(gated, j)

    for h in range(halves):
        gate = branch(gated, h * part, part)
        for g in range(groups):
            y_wait(h, g)
        rows = pl.ds(h * part, part)
        convolved = jnp.transpose(y_got[h].astype(jnp.float32).reshape(width, part))
        out_ref[rows, :] = (gate * (convolved + direct[rows, :])).astype(jnp.bfloat16)

    @pl.when(end)
    def _():
        for i in range(3):
            for b in range(2):
                weight_copy(i, b, False).wait_send()
        for q in every:
            token_copy(0, q, 0).wait_send()

    @pl.when(middle)
    def _():
        for q in every:
            token_copy(0, q, 0).wait_send()
            token_copy(0, q, 1).wait_send()
            token_copy(1, q, 0).wait_send()
        for q in plain:
            token_copy(2, q, 1).wait_send()
            token_copy(3, q, 1).wait_send()
        for i in range(3):

            def go(shift, _):
                mate_copy(i, shift, place).wait_send()
                return 0

            lax.fori_loop(1, mates, go, 0)
            twin_copy(i, core).wait_send()
            for r in range(1, chunks):
                partial_copy(i, r, -1).wait_send()

    for shift in range(1, tp_count):
        square_copy(shift, t).wait_send()
    sent_to_peers(f_sent, f_got, f_send, f_recv)
    for j in range(chunks):
        sent_to_peers(*x_refs(j))
    for h in range(halves):
        for g in range(groups):
            y_sent_all(h, g)


def body(tokens, norm_gain, proj_weight, short_taps, long_filter, skip_gain):
    part_count, tp_count = lax.axis_size("ctx"), lax.axis_size("tp")
    row_count, width = long_filter.shape
    features = tokens.shape[1]
    channels = width // part_count
    chunk, halves = 128, 2
    groups = 2 if channels % (2 * EDGE) == 0 else 1
    each = channels // groups
    chunks, pieces = row_count // chunk, row_count // chunk + 1
    rows = (part_count + 1) * channels
    cos, sin = twist_tables(part_count, row_count)
    forward, backward = inner_tables(row_count, halves)
    held = pl.BlockSpec(memory_space=pltpu.VMEM)
    away = pl.BlockSpec(memory_space=pl.ANY)
    bf16, f32 = jnp.bfloat16, jnp.float32
    dma = pltpu.SemaphoreType.DMA
    part = row_count // halves
    return pl.pallas_call(
        functools.partial(block_kernel, part_count, tp_count, chunk, halves, groups),
        out_shape=jax.ShapeDtypeStruct((row_count, width), bf16),
        in_specs=[away, held, away, held, away, held, held, held, away, away],
        out_specs=held,
        scratch_shapes=[
            pltpu.VMEM((tp_count, row_count, features), bf16),
            pltpu.VMEM(proj_weight.shape, bf16),
            pltpu.VMEM((3, row_count, width), f32),
            pltpu.VMEM((3, row_count, features), bf16),
            pltpu.VMEM((row_count, 128), f32),
            pltpu.VMEM((tp_count, 8, row_count), f32),
            pltpu.VMEM((row_count, width), f32),
            pltpu.VMEM((part_count, channels, row_count), bf16),
            pltpu.VMEM((part_count, channels, row_count), bf16),
            pltpu.VMEM((rows, 2 * row_count), bf16),
            pltpu.VMEM((rows, 2 * row_count), f32),
            pltpu.VMEM((rows, 2 * row_count), bf16),
            pltpu.VMEM((3, EDGE, width), bf16),
            pltpu.VMEM((3, EDGE, width), bf16),
            pltpu.VMEM((3, row_count + 8, width), f32),
            pltpu.VMEM((row_count, width), f32),
            pltpu.VMEM((chunks, part_count, channels, chunk), bf16),
            pltpu.VMEM((chunks, part_count, channels, chunk), bf16),
            pltpu.VMEM((halves, (part_count + 1) * each, 2 * part), f32),
            pltpu.VMEM((halves, part_count, groups, each, part), bf16),
            pltpu.VMEM((halves, part_count, groups, each, part), bf16),
            pltpu.VMEM(forward.shape, bf16),
            pltpu.VMEM(backward.shape, bf16),
            pltpu.VMEM((3, 2, part_count // 2, 2, features // part_count, width), bf16),
            pltpu.VMEM((chunks - 1, 3, chunk, width), bf16),
            pltpu.VMEM((chunks - 1, 3, chunk, width), bf16),
            dma((4,)),
            dma((tp_count,)),
            dma((2, tp_count, pieces)),
            dma((tp_count, pieces)),
            dma((tp_count,)),
            dma((tp_count,)),
            dma((part_count,)),
            dma((part_count,)),
            dma((2,)),
            dma((chunks, part_count)),
            dma((chunks, part_count)),
            dma((halves, groups, part_count)),
            dma((halves, groups, part_count)),
            dma((3, 2)),
            dma((3, 2)),
            dma((3, part_count // 2)),
            dma((3, part_count // 2)),
            dma((3,)),
            dma((3,)),
            dma((chunks - 1, 3)),
            dma((chunks - 1, 3)),
        ],
        compiler_params=pltpu.CompilerParams(
            vmem_limit_bytes=60 << 20, collective_id=0, has_side_effects=True
        ),
        name="hyena_block",
    )(
        tokens, norm_gain.reshape(tp_count, 1, features), proj_weight, short_taps, long_filter,
        skip_gain[None, :], cos, sin, forward, backward,
    )


def solution(mesh):
    placed = (
        P("ctx", "tp"),
        P(),
        P(None, None, "tp"),
        P(None, None, "tp"),
        P("ctx", "tp"),
        P("tp"),
    )
    return jax.shard_map(
        body, mesh=mesh, in_specs=placed, out_specs=P("ctx", "tp"), check_vma=False
    )
```

```python
import functools
import math

import jax
import jax.numpy as jnp
import numpy as np
from jax import lax
from jax.experimental import pallas as pl
from jax.experimental.pallas import tpu as pltpu
from jax.sharding import PartitionSpec as P

MESH = pl.DeviceIdType.MESH
EDGE = 16


def twist_tables(part_count, row_count):
    turn = np.arange(part_count + 1)[:, None] * np.arange(row_count)[None, :]
    angles = turn * (math.pi / (part_count * row_count))
    return np.cos(angles).astype(np.float32), np.sin(angles).astype(np.float32)


def inner_tables(row_count, halves):
    turn = np.arange(row_count)[:, None] * np.arange(row_count)[None, :] % row_count
    angles = turn * (2.0 * math.pi / row_count)
    cos, sin = np.cos(angles), np.sin(angles)
    forward = np.block([[cos, -sin], [sin, cos]])
    backward = np.block([[cos, sin], [-sin, cos]])
    part = row_count // halves
    backward = np.stack(
        [
            np.concatenate(
                [
                    backward[:, h * part : (h + 1) * part],
                    backward[:, row_count + h * part : row_count + (h + 1) * part],
                ],
                axis=1,
            )
            for h in range(halves)
        ]
    )
    return forward.astype(jnp.bfloat16), backward.astype(jnp.bfloat16)


def turn_of(a, k, part_count):
    step = a * k % (2 * part_count)
    cos = math.cos(math.pi * step / part_count)
    sin = math.sin(math.pi * step / part_count)
    return (0.0 if abs(cos) < 1e-12 else cos, 0.0 if abs(sin) < 1e-12 else sin)


def weighted(terms):
    total = None
    for factor, term in terms:
        if factor == 0.0:
            continue
        scaled = term if abs(factor - 1.0) < 1e-12 else -term if abs(factor + 1.0) < 1e-12 else factor * term
        total = scaled if total is None else total + scaled
    return total


def block_kernel(
    part_count, tp_count, chunk, halves, groups,
    tokens_any, gain_ref, weight_any, taps_ref, filter_any, skip_ref, cos_ref, sin_ref, forward_any, backward_any,
    out_ref,
    held, weight, total, normed, scale, squares, filt, f_sent, f_got, turned, response, spec_turned,
    halo_out, halo_in, wide, direct, x_sent, x_got, back, y_sent, y_got, forward, backward, lent, p_sent, p_got,
    load_sem, weight_sem, tok_send, tok_recv, sq_send, sq_recv, f_send, f_recv, halo_sem, x_send, x_recv, y_send, y_recv,
    w_send, w_recv, wp_send, wp_recv, wc_send, wc_recv, p_send, p_recv,
):
    row_count, width = out_ref.shape
    features = held.shape[2]
    channels = width // part_count
    each = channels // groups
    span = (part_count + 1) * each
    chunks = row_count // chunk
    share = features // part_count
    mates = part_count // 2
    me = lax.axis_index("ctx")
    t = lax.axis_index("tp")
    place, core = me // 2, lax.rem(me, 2)
    upper = t // (tp_count // 2)
    u = t + upper * (tp_count - 1 - 2 * t)
    inward = 1 - 2 * upper
    middle = u == 1
    end = u == 0

    def mirrored(o):
        return o + upper * (tp_count - 1 - 2 * o)

    order = [t, mirrored(1 - u), mirrored(2), mirrored(3)]
    slots = (2, 2, 0, 1)
    first, gated = (1, 2), 0

    loads = [
        pltpu.make_async_copy(source, target, load_sem.at[i])
        for i, (source, target) in enumerate(
            [
                (tokens_any, held.at[t]),
                (filter_any, filt),
                (forward_any, forward),
                (backward_any, backward),
            ]
        )
    ]

    def block(k):
        return pl.ds(pl.multiple_of(order[k] * features, features), features)

    def weight_load(k):
        return pltpu.make_async_copy(weight_any.at[:, block(k), :], weight.at[:, block(k), :], weight_sem.at[k])

    barrier = pltpu.get_barrier_semaphore()

    def greet_ctx(shift, _):
        pl.semaphore_signal(barrier, inc=1, device_id={"ctx": lax.rem(me + shift, part_count)}, device_id_type=MESH)
        return 0

    lax.fori_loop(1, part_count, greet_ctx, 0)
    for shift in range(1, tp_count):
        pl.semaphore_signal(barrier, inc=1, device_id={"tp": lax.rem(t + shift, tp_count)}, device_id_type=MESH)
    loads[0].start()
    loads[1].start()
    pl.semaphore_wait(barrier, part_count - 1 + tp_count - 1)

    pieces = (
        [(row_count - EDGE, EDGE)]
        + [(j * chunk, chunk) for j in range(chunks - 1)]
        + [((chunks - 1) * chunk, chunk - EDGE)]
    )
    every = range(len(pieces))
    plain = (0, 1)

    def token_copy(k, q, way):
        rows = pl.ds(*pieces[q])
        source = tokens_any.at[rows, :] if k == 0 else held.at[order[k], rows, :]
        return pltpu.make_async_remote_copy(
            src_ref=source,
            dst_ref=held.at[order[k], rows, :],
            send_sem=tok_send.at[way, k, q],
            recv_sem=tok_recv.at[order[k], q],
            device_id={"tp": t + (inward if way == 0 else -inward)},
            device_id_type=MESH,
        )

    def weight_copy(i, b, local):
        rows = pl.ds(pl.multiple_of(order[2 + b] * features + me * share, share), share)
        target = lent.at[i, b, place, core]
        return pltpu.make_async_remote_copy(
            src_ref=target if local else weight_any.at[i, rows, :],
            dst_ref=target,
            send_sem=w_send.at[i, b],
            recv_sem=w_recv.at[i, b],
            device_id={"tp": t + inward},
            device_id_type=MESH,
        )

    def mate_copy(i, shift, slot):
        return pltpu.make_async_remote_copy(
            src_ref=lent.at[i, :, slot, core],
            dst_ref=lent.at[i, :, slot, core],
            send_sem=wp_send.at[i, shift],
            recv_sem=wp_recv.at[i, slot],
            device_id={"ctx": lax.rem(me + 2 * shift, part_count)},
            device_id_type=MESH,
        )

    def twin_copy(i, side):
        return pltpu.make_async_remote_copy(
            src_ref=lent.at[i, :, :, side],
            dst_ref=lent.at[i, :, :, side],
            send_sem=wc_send.at[i],
            recv_sem=wc_recv.at[i],
            device_id={"ctx": me + 1 - 2 * core},
            device_id_type=MESH,
        )

    def partial_copy(i, r, way):
        return pltpu.make_async_remote_copy(
            src_ref=p_sent.at[r - 1, i],
            dst_ref=p_got.at[r - 1, i],
            send_sem=p_send.at[r - 1, i],
            recv_sem=p_recv.at[r - 1, i],
            device_id={"tp": t + way * inward},
            device_id_type=MESH,
        )

    @pl.when(end)
    def _():
        for b in range(2):
            weight_copy(first[0], b, False).start()

    @pl.when(middle)
    def _():
        for q in plain:
            token_copy(0, q, 0).start()
            token_copy(0, q, 1).start()

    loads[0].wait()
    own = held[t].astype(jnp.float32)
    sums = jnp.sum(own * own, axis=1, keepdims=True)
    squares[t] = jnp.transpose(jnp.broadcast_to(sums, (row_count, 128)))[:8]

    def square_copy(shift, slot):
        return pltpu.make_async_remote_copy(
            src_ref=squares.at[slot],
            dst_ref=squares.at[slot],
            send_sem=sq_send.at[shift],
            recv_sem=sq_recv.at[slot],
            device_id={"tp": lax.rem(t + shift, tp_count)},
            device_id_type=MESH,
        )

    for shift in range(1, tp_count):
        square_copy(shift, t).start()

    @pl.when(end)
    def _():
        for b in range(2):
            weight_copy(first[1], b, False).start()
        for q in every:
            if q == 4:
                for b in range(2):
                    weight_copy(gated, b, False).start()
            token_copy(0, q, 0).start()

    @pl.when(middle)
    def _():
        for q in every:
            if q not in plain:
                token_copy(0, q, 1).start()
                token_copy(0, q, 0).start()

    for k in range(tp_count):
        weight_load(k).start()
    loads[2].start()
    loads[3].start()

    def peer_copy(shift, source, target, send_sem, recv_sem):
        peer = lax.rem(me + shift, part_count)
        return pltpu.make_async_remote_copy(
            src_ref=source.at[peer],
            dst_ref=target.at[me],
            send_sem=send_sem.at[peer],
            recv_sem=recv_sem.at[me],
            device_id={"ctx": peer},
            device_id_type=MESH,
        )

    def send_to_peers(*refs):
        def go(shift, _):
            peer_copy(shift, *refs).start()
            return 0

        lax.fori_loop(1, part_count, go, 0)

    def sent_to_peers(*refs):
        def go(shift, _):
            peer_copy(shift, *refs).wait_send()
            return 0

        lax.fori_loop(1, part_count, go, 0)

    def wait_for_peers(source, target, send_sem, recv_sem):
        def go(shift, _):
            peer = lax.rem(me + shift, part_count)
            pltpu.make_async_remote_copy(
                src_ref=source.at[peer],
                dst_ref=target.at[peer],
                send_sem=send_sem.at[peer],
                recv_sem=recv_sem.at[peer],
                device_id={"ctx": peer},
                device_id_type=MESH,
            ).wait_recv()
            return 0

        lax.fori_loop(1, part_count, go, 0)

    loads[1].wait()
    group = max(128, channels)
    for j in range(width // group):
        columns = pl.ds(j * group, group)
        blocks = group // channels
        f_sent[pl.ds(j * blocks, blocks)] = (
            jnp.transpose(filt[:, columns]).astype(jnp.bfloat16).reshape(blocks, channels, row_count)
        )
    f_got[me] = f_sent[me]
    send_to_peers(f_sent, f_got, f_send, f_recv)

    def row_scales():
        for shift in range(1, tp_count):
            square_copy(shift, lax.rem(t + shift, tp_count)).wait_recv()
        mean = (squares[0] + squares[1] + squares[2] + squares[3]) * (1.0 / (tp_count * features))
        inverse = lax.rsqrt(mean + 1e-06)
        scale[...] = jnp.transpose(jnp.broadcast_to(inverse[:1], (128, row_count)))

    def normalise(k, start, size):
        rows = pl.ds(start, size)
        values = held[order[k], rows, :].astype(jnp.float32) * scale[rows, :1] * gain_ref[order[k]]
        normed[slots[k], rows, :] = values.astype(jnp.bfloat16)

    def product(k, i, rows):
        return jnp.dot(normed[slots[k], rows, :], weight[i, block(k), :], preferred_element_type=jnp.float32)

    def accumulate(k):
        def one(i, _):
            added = product(k, i, slice(None))
            total[i] = added if k == 0 else total[i] + added
            return 0

        weight_load(k).wait()
        lax.fori_loop(0, 3, one, 0)

    def outer(parts, lanes, high):
        for k in range(part_count + 1):
            turns = [turn_of(a, k, part_count) for a in range(part_count)]
            cos, sin = cos_ref[pl.ds(k, 1), lanes], sin_ref[pl.ds(k, 1), lanes]
            real = weighted([(c[0], p) for c, p in zip(turns, parts)])
            imag = weighted([(-c[1], p) for c, p in zip(turns, parts)])
            if imag is None:
                low_value, high_value = real * cos, -real * sin
            else:
                low_value, high_value = real * cos + imag * sin, imag * cos - real * sin
            for g in range(groups):
                rows = pl.ds(g * span + k * each, each)
                turned[rows, lanes] = low_value[g * each : (g + 1) * each].astype(jnp.bfloat16)
                turned[rows, high] = high_value[g * each : (g + 1) * each].astype(jnp.bfloat16)

    def filter_spectrum():
        wait_for_peers(f_sent, f_got, f_send, f_recv)

        def one(j, _):
            lanes = pl.ds(pl.multiple_of(j * chunk, chunk), chunk)
            high = pl.ds(pl.multiple_of(row_count + j * chunk, chunk), chunk)
            outer([f_got[a, :, lanes].astype(jnp.float32) for a in range(part_count)], lanes, high)
            return 0

        lax.fori_loop(0, chunks, one, 0)
        loads[2].wait()
        loads[3].wait()
        unit = 1.0 / (2 * part_count * row_count)
        response[...] = jnp.dot(turned[...], forward[...], preferred_element_type=jnp.float32) * (2.0 * unit)
        for g in range(groups):
            for k in (0, part_count):
                rows = pl.ds(g * span + k * each, each)
                response[rows, :] = response[rows, :] * 0.5

    def arrived(k, q):
        token_copy(k, q, 0).wait_recv()

    edge = pl.ds(row_count - EDGE, EDGE)
    halo = pltpu.make_async_remote_copy(
        src_ref=halo_out,
        dst_ref=halo_in,
        send_sem=halo_sem.at[0],
        recv_sem=halo_sem.at[1],
        device_id={"ctx": lax.rem(me + 1, part_count)},
        device_id_type=MESH,
    )

    def take_halo():
        halo.wait()
        for i in range(3):
            before = halo_in[i].astype(jnp.float32)[EDGE - 8 :]
            wide[i, pl.ds(0, 8), :] = jnp.where(me > 0, before, jnp.zeros_like(before))

    def widen(i, j):
        projected = total[i, pl.ds(j * chunk, chunk), :].astype(jnp.bfloat16)
        wide[i, pl.ds(8 + j * chunk, chunk), :] = projected.astype(jnp.float32)

    def branch(i, start, size):
        return (
            taps_ref[i, pl.ds(0, 1), :] * wide[i, pl.ds(8 + start, size), :]
            + taps_ref[i, pl.ds(1, 1), :] * wide[i, pl.ds(7 + start, size), :]
            + taps_ref[i, pl.ds(2, 1), :] * wide[i, pl.ds(6 + start, size), :]
        )

    def x_refs(j):
        return x_sent.at[j], x_got.at[j], x_send.at[j], x_recv.at[j]

    def send_signal(j):
        mixed = branch(1, j * chunk, chunk) * branch(2, j * chunk, chunk)
        x_sent[j] = jnp.transpose(mixed).astype(jnp.bfloat16).reshape(part_count, channels, chunk)
        send_to_peers(*x_refs(j))
        x_got[j, me] = x_sent[j, me]
        direct[pl.ds(j * chunk, chunk), :] = skip_ref[...] * mixed

    def take_signal(j):
        wait_for_peers(*x_refs(j))
        lanes, high = pl.ds(j * chunk, chunk), pl.ds(row_count + j * chunk, chunk)
        outer([x_got[j, a].astype(jnp.float32) for a in range(part_count)], lanes, high)

    @pl.when(middle)
    def _():
        def share_out(i):
            for b in range(2):
                weight_copy(i, b, True).wait_recv()

            def go(shift, _):
                mate_copy(i, shift, place).start()
                return 0

            lax.fori_loop(1, mates, go, 0)

        def to_twin(i):
            def go(shift, _):
                mate_copy(i, shift, lax.rem(place + shift, mates)).wait_recv()
                return 0

            lax.fori_loop(1, mates, go, 0)
            twin_copy(i, core).start()

        def partial(i, r):
            rows = pl.ds(r * chunk, chunk)
            value = None
            for b in range(2):
                matrix = lent[i, b].reshape(features, width)
                part = jnp.dot(normed[b, rows, :], matrix, preferred_element_type=jnp.float32)
                value = part if value is None else value + part
            p_sent[r - 1, i] = value.astype(jnp.bfloat16)
            partial_copy(i, r, -1).start()

        def inward_piece(q):
            arrived(1, q)
            token_copy(1, q, 0).start()

        def add_far(i, rows):
            total[i, rows, :] = total[i, rows, :] + product(3, i, rows)

        share_out(first[0])
        for q in plain:
            arrived(2, q)
            token_copy(2, q, 1).start()
        share_out(first[1])
        row_scales()
        normalise(0, 0, row_count)
        accumulate(0)
        for q in plain:
            inward_piece(q)
        filter_spectrum()
        to_twin(first[0])
        inward_piece(2)
        for q in plain:
            arrived(3, q)
            token_copy(3, q, 1).start()
        normalise(3, 0, chunk)
        for q in range(2, len(pieces) - 1):
            arrived(2, q)
        normalise(2, 0, row_count - chunk)
        inward_piece(3)
        to_twin(first[1])
        twin_copy(first[0], 1 - core).wait_recv()
        weight_load(3).wait()
        for r in range(1, chunks):
            arrived(3, r + 1)
            normalise(3, r * chunk, chunk)
            if r == 1:
                twin_copy(first[1], 1 - core).wait_recv()
            for i in first:
                partial(i, r)
            if r == 1:
                share_out(gated)
                arrived(2, len(pieces) - 1)
                normalise(2, row_count - chunk, chunk)
                accumulate(2)
            if r == chunks - 2:
                inward_piece(len(pieces) - 1)
                normalise(1, 0, row_count)
                accumulate(1)
                for i in first:
                    add_far(i, pl.ds(0, row_count - chunk))
                    for j in range(chunks - 1):
                        widen(i, j)
        for j in range(1, chunks - 1):
            send_signal(j)
        last = pl.ds(row_count - chunk, chunk)
        for i in range(3):
            add_far(i, last)
            halo_out[i] = total[i, edge, :].astype(jnp.bfloat16)
        halo.start()
        for i in first:
            widen(i, chunks - 1)
        send_signal(chunks - 1)
        to_twin(gated)
        take_halo()
        send_signal(0)
        add_far(gated, pl.ds(0, row_count - chunk))
        twin_copy(gated, 1 - core).wait_recv()
        for r in range(1, chunks):
            partial(gated, r)
        for j in range(1, chunks):
            take_signal(j)
        take_signal(0)

    @pl.when(end)
    def _():
        row_scales()
        normalise(0, 0, row_count)
        accumulate(0)
        filter_spectrum()
        for q in every:
            arrived(1, q)
        normalise(1, 0, row_count)
        accumulate(1)
        for k in (2, 3):
            weight_load(k).wait()
            arrived(k, 0)
            normalise(k, row_count - EDGE, EDGE)
        for i in range(3):
            halo_out[i] = (total[i, edge, :] + product(2, i, edge) + product(3, i, edge)).astype(jnp.bfloat16)
        halo.start()
        for k in (2, 3):
            arrived(k, 1)
            normalise(k, 0, chunk)
        rows = pl.ds(0, chunk)
        for i in range(3):
            total[i, rows, :] = total[i, rows, :] + product(2, i, rows) + product(3, i, rows)
        take_halo()
        for j in range(chunks):
            for i in first:
                if j > 0:
                    rows = pl.ds(j * chunk, chunk)
                    partial_copy(i, j, 1).wait_recv()
                    total[i, rows, :] = total[i, rows, :] + p_got[j - 1, i].astype(jnp.float32)
                widen(i, j)
            send_signal(j)
            if j > 0:
                take_signal(j - 1)
        take_signal(chunks - 1)

    part = row_count // halves

    def y_copy(h, g, shift):
        peer = lax.rem(me + shift, part_count)
        return pltpu.make_async_remote_copy(
            src_ref=y_sent.at[h, peer, g],
            dst_ref=y_got.at[h, me, g],
            send_sem=y_send.at[h, g, peer],
            recv_sem=y_recv.at[h, g, me],
            device_id={"ctx": peer},
            device_id_type=MESH,
        )

    def y_start(h, g):
        def go(shift, _):
            y_copy(h, g, shift).start()
            return 0

        lax.fori_loop(1, part_count, go, 0)

    def y_sent_all(h, g):
        def go(shift, _):
            y_copy(h, g, shift).wait_send()
            return 0

        lax.fori_loop(1, part_count, go, 0)

    def y_wait(h, g):
        def go(shift, _):
            peer = lax.rem(me + shift, part_count)
            pltpu.make_async_remote_copy(
                src_ref=y_sent.at[h, peer, g],
                dst_ref=y_got.at[h, peer, g],
                send_sem=y_send.at[h, g, peer],
                recv_sem=y_recv.at[h, g, peer],
                device_id={"ctx": peer},
                device_id_type=MESH,
            ).wait_recv()
            return 0

        lax.fori_loop(1, part_count, go, 0)

    step = row_count // 2
    for g in range(groups):
        mine = pl.ds(g * span, span)
        for n in range(2):
            low, high = pl.ds(n * step, step), pl.ds(row_count + n * step, step)
            real = jnp.dot(turned[mine, :], forward[:, low], preferred_element_type=jnp.float32)
            imag = jnp.dot(turned[mine, :], forward[:, high], preferred_element_type=jnp.float32)
            gain_real, gain_imag = response[mine, low], response[mine, high]
            spec_turned[mine, low] = (real * gain_real - imag * gain_imag).astype(jnp.bfloat16)
            spec_turned[mine, high] = (real * gain_imag + imag * gain_real).astype(jnp.bfloat16)
        for h in range(halves):
            back[h] = jnp.dot(spec_turned[mine, :], backward[h], preferred_element_type=jnp.float32)
            lanes = pl.ds(h * part, part)
            low, high = pl.ds(0, part), pl.ds(part, part)
            for k in range(part_count + 1):
                cos, sin = cos_ref[pl.ds(k, 1), lanes], sin_ref[pl.ds(k, 1), lanes]
                rows = pl.ds(k * each, each)
                real, imag = back[h, rows, low], back[h, rows, high]
                back[h, rows, low] = real * cos - imag * sin
                if 0 < k < part_count:
                    back[h, rows, high] = real * sin + imag * cos
            for a in range(part_count):
                terms = []
                for k in range(part_count + 1):
                    cos, sin = turn_of(a, k, part_count)
                    rows = pl.ds(k * each, each)
                    terms.append((cos, back[h, rows, low]))
                    if sin != 0.0:
                        terms.append((-sin, back[h, rows, high]))
                y_sent[h, a, g] = weighted(terms).astype(jnp.bfloat16)
            y_start(h, g)
            y_got[h, me, g] = y_sent[h, me, g]

    @pl.when(end)
    def _():
        for j in range(1, chunks):
            rows = pl.ds(j * chunk, chunk)
            partial_copy(gated, j, 1).wait_recv()
            total[gated, rows, :] = total[gated, rows, :] + p_got[j - 1, gated].astype(jnp.float32)

    for j in range(chunks):
        widen(gated, j)

    for h in range(halves):
        gate = branch(gated, h * part, part)
        for g in range(groups):
            y_wait(h, g)
        rows = pl.ds(h * part, part)
        convolved = jnp.transpose(y_got[h].astype(jnp.float32).reshape(width, part))
        out_ref[rows, :] = gate * (convolved + direct[rows, :])

    @pl.when(end)
    def _():
        for i in range(3):
            for b in range(2):
                weight_copy(i, b, False).wait_send()
        for q in every:
            token_copy(0, q, 0).wait_send()

    @pl.when(middle)
    def _():
        for q in every:
            token_copy(0, q, 0).wait_send()
            token_copy(0, q, 1).wait_send()
            token_copy(1, q, 0).wait_send()
        for q in plain:
            token_copy(2, q, 1).wait_send()
            token_copy(3, q, 1).wait_send()
        for i in range(3):

            def go(shift, _):
                mate_copy(i, shift, place).wait_send()
                return 0

            lax.fori_loop(1, mates, go, 0)
            twin_copy(i, core).wait_send()
            for r in range(1, chunks):
                partial_copy(i, r, -1).wait_send()

    for shift in range(1, tp_count):
        square_copy(shift, t).wait_send()
    sent_to_peers(f_sent, f_got, f_send, f_recv)
    for j in range(chunks):
        sent_to_peers(*x_refs(j))
    for h in range(halves):
        for g in range(groups):
            y_sent_all(h, g)


def body(tokens, norm_gain, proj_weight, short_taps, long_filter, skip_gain):
    part_count, tp_count = lax.axis_size("ctx"), lax.axis_size("tp")
    row_count, width = long_filter.shape
    features = tokens.shape[1]
    channels = width // part_count
    chunk, halves = 128, 2
    groups = 2 if channels % (2 * EDGE) == 0 else 1
    each = channels // groups
    chunks, pieces = row_count // chunk, row_count // chunk + 1
    rows = (part_count + 1) * channels
    cos, sin = twist_tables(part_count, row_count)
    forward, backward = inner_tables(row_count, halves)
    held = pl.BlockSpec(memory_space=pltpu.VMEM)
    away = pl.BlockSpec(memory_space=pl.ANY)
    bf16, f32 = jnp.bfloat16, jnp.float32
    dma = pltpu.SemaphoreType.DMA
    part = row_count // halves
    return pl.pallas_call(
        functools.partial(block_kernel, part_count, tp_count, chunk, halves, groups),
        out_shape=jax.ShapeDtypeStruct((row_count, width), f32),
        in_specs=[away, held, away, held, away, held, held, held, away, away],
        out_specs=held,
        scratch_shapes=[
            pltpu.VMEM((tp_count, row_count, features), bf16),
            pltpu.VMEM(proj_weight.shape, bf16),
            pltpu.VMEM((3, row_count, width), f32),
            pltpu.VMEM((3, row_count, features), bf16),
            pltpu.VMEM((row_count, 128), f32),
            pltpu.VMEM((tp_count, 8, row_count), f32),
            pltpu.VMEM((row_count, width), f32),
            pltpu.VMEM((part_count, channels, row_count), bf16),
            pltpu.VMEM((part_count, channels, row_count), bf16),
            pltpu.VMEM((rows, 2 * row_count), bf16),
            pltpu.VMEM((rows, 2 * row_count), f32),
            pltpu.VMEM((rows, 2 * row_count), bf16),
            pltpu.VMEM((3, EDGE, width), bf16),
            pltpu.VMEM((3, EDGE, width), bf16),
            pltpu.VMEM((3, row_count + 8, width), f32),
            pltpu.VMEM((row_count, width), f32),
            pltpu.VMEM((chunks, part_count, channels, chunk), bf16),
            pltpu.VMEM((chunks, part_count, channels, chunk), bf16),
            pltpu.VMEM((halves, (part_count + 1) * each, 2 * part), f32),
            pltpu.VMEM((halves, part_count, groups, each, part), bf16),
            pltpu.VMEM((halves, part_count, groups, each, part), bf16),
            pltpu.VMEM(forward.shape, bf16),
            pltpu.VMEM(backward.shape, bf16),
            pltpu.VMEM((3, 2, part_count // 2, 2, features // part_count, width), bf16),
            pltpu.VMEM((chunks - 1, 3, chunk, width), bf16),
            pltpu.VMEM((chunks - 1, 3, chunk, width), bf16),
            dma((4,)),
            dma((tp_count,)),
            dma((2, tp_count, pieces)),
            dma((tp_count, pieces)),
            dma((tp_count,)),
            dma((tp_count,)),
            dma((part_count,)),
            dma((part_count,)),
            dma((2,)),
            dma((chunks, part_count)),
            dma((chunks, part_count)),
            dma((halves, groups, part_count)),
            dma((halves, groups, part_count)),
            dma((3, 2)),
            dma((3, 2)),
            dma((3, part_count // 2)),
            dma((3, part_count // 2)),
            dma((3,)),
            dma((3,)),
            dma((chunks - 1, 3)),
            dma((chunks - 1, 3)),
        ],
        compiler_params=pltpu.CompilerParams(
            vmem_limit_bytes=60 << 20, collective_id=0, has_side_effects=True
        ),
        name="hyena_block",
    )(
        tokens, norm_gain.reshape(tp_count, 1, features), proj_weight, short_taps, long_filter,
        skip_gain[None, :], cos, sin, forward, backward,
    ).astype(bf16)


def solution(mesh):
    placed = (
        P("ctx", "tp"),
        P(),
        P(None, None, "tp"),
        P(None, None, "tp"),
        P("ctx", "tp"),
        P("tp"),
    )
    return jax.shard_map(
        body, mesh=mesh, in_specs=placed, out_specs=P("ctx", "tp"), check_vma=False
    )
```
